512 devices in a mesh: swath: 32 (over z, core), chan: 16 (over x, y).
Axes of the slice: x: 4, y: 4, z: 16, core: 2. Of those that a mesh axis runs over, the one named last changes fastest.
Arguments:
- grid_profiles: bfloat16 [32768, 256], P('swath'), may hold values from -6 to 6
- send_lists: int32 [32, 32, 128], P('swath'), may hold values from 0 to 1023
- counts: int32 [32, 32], P('swath'), may hold values from 1 to 128, as said below
- angle_index: int32 [128], replicated, may hold values from 0 to 7
- jacobian: bfloat16 [3, 256, 608], P(None, None, 'chan'), may hold values from -0.375 to 0.375
- observed: bfloat16 [608, 131072], P('chan', 'swath'), may hold values from -6 to 6
- kappa: float32 [2, 608], P(None, 'chan'), may hold values from 0.04 to 0.24
- factor: bfloat16 [608, 608], P('chan')
Outputs:
- weighted: float32 [608, 131072], P('chan', 'swath')
The draws below stay inside these ranges and needn't reach their ends.
Inputs may be any that keep to these rules, and one draw needn't show every extreme that they name: `counts`: some receiver gets 128 live slots from every sender; every entry is at least one.
All inputs are finite; a program needn't handle non-finite values.
Results may differ from the reference program's by a relative error of at most 0.0029.
Values may be sent and summed in bfloat16 or wider, within the bound.
A program may use at most 64 MiB of HBM per device.

```python
import math
import jax
import jax.numpy as jnp

CHAN = 608
PROF = 256
XTRACK = 128
NANG = 8
GROWS_DEV = 1024
CAP = 128
NPIX = 131072
NLINES = 1024
GROWS = 32768
N_SWATH = 32


def draw_counts(key, part):
    first_key, second_key = jax.random.split(key)
    order = jax.random.permutation(first_key, N_SWATH)
    full_receiver = order < max(1, N_SWATH // 4)
    lowest = max(1, CAP // 6)
    highest = max(lowest + 1, CAP // 2 + 1)
    random_counts = jax.random.randint(second_key, (N_SWATH, N_SWATH), lowest, highest)
    return jnp.where(full_receiver[None, :], CAP, random_counts).astype(jnp.int32)


def draw_factor(key, part):
    first_key, second_key = jax.random.split(key)
    row_index = jnp.arange(CHAN)[:, None]
    col_index = jnp.arange(CHAN)[None, :]
    noise = jax.random.normal(first_key, (CHAN, CHAN), jnp.float32)
    lower = noise * 0.8 / jnp.sqrt((row_index + 1).astype(jnp.float32))
    diagonal = jnp.exp(jax.random.uniform(second_key, (CHAN,), jnp.float32, -0.5, 0.5))
    matrix = jnp.where(row_index > col_index, lower, 0.0)
    matrix = jnp.where(row_index == col_index, diagonal[:, None], matrix)
    return matrix.astype(jnp.bfloat16)


def touch_ends(drawn, key, smallest, largest):
    dims = drawn.shape
    index_at = [jax.random.randint(jax.random.fold_in(key, axis), (), 0, dims[axis]) for axis in range(len(dims))]
    drawn = drawn.at[tuple(index_at)].set(smallest)
    longest = dims.index(max(dims))
    index_at[longest] = (index_at[longest] + 1) % dims[longest]
    return drawn.at[tuple(index_at)].set(largest)


def shard_levels(stream_key, extent, cuts, low, largest):
    factor_of, own = 1.0, jax.random.fold_in(stream_key, 6)
    for position, parts in cuts:
        heights = jnp.exp(jax.random.uniform(jax.random.fold_in(own, position), (parts,), jnp.float32, low / len(cuts), largest / len(cuts)))
        factor_of = factor_of * jnp.repeat(heights, extent[position] // parts).reshape([-1 if axis == position else 1 for axis in range(len(extent))])
    return factor_of


def scatter_about(rng, extent, scale, limit, pieces=(), held_as=jnp.bfloat16):
    drawn = jax.random.normal(rng, extent, jnp.float32) * scale
    if len(pieces) > 0:
        drawn = shard_levels(rng, extent, pieces, -0.22, 0.18) * drawn
    return jnp.clip(drawn, min=-limit, max=limit).astype(held_as)


def setup_inputs(seed: int = 0) -> dict:
    key_of = jax.random.split(jax.random.key(seed), 9)
    return {
        "grid_profiles": scatter_about(key_of[0], (GROWS, PROF), 1.0, 6.0, ((0, 32),)),
        "send_lists": touch_ends(jax.random.randint(key_of[1], (N_SWATH, N_SWATH, CAP), 0, GROWS_DEV), jax.random.fold_in(key_of[1], 1), 0, GROWS_DEV - 1).astype(jnp.int32),
        "counts": draw_counts(jax.random.fold_in(key_of[8], 71), 0),
        "angle_index": touch_ends(jax.random.randint(key_of[3], (XTRACK,), 0, NANG), jax.random.fold_in(key_of[3], 1), 0, NANG - 1).astype(jnp.int32),
        "jacobian": scatter_about(key_of[4], (3, PROF, CHAN), PROF ** -0.5, 0.375, ((2, 16),)),
        "observed": scatter_about(key_of[5], (CHAN, NPIX), 1.0, 6.0, ((0, 16), (1, 32))),
        "kappa": jnp.clip(jnp.exp(math.log(0.24) - 1.7917595 * jax.random.uniform(key_of[6], (2, CHAN), jnp.float32) ** shard_levels(key_of[6], (2, CHAN), ((1, 16),), -0.2, 0.2)), 0.04, 0.24),
        "factor": draw_factor(jax.random.fold_in(key_of[8], 71), 0),
    }


max_zenith = math.pi / 3.0


def fetch_rows(grid_block, row_picks):
    return grid_block[row_picks]


def reference(grid_profiles, send_lists, counts, angle_index, jacobian, observed, kappa, factor):
    grid_r = grid_profiles.reshape(N_SWATH, GROWS_DEV, PROF)
    fetched = jax.vmap(fetch_rows)(grid_r, send_lists)
    live_slot = jnp.arange(CAP, dtype=jnp.int32)[None, None, :] < counts[:, :, None]
    fetched = jnp.where(live_slot[..., None], fetched, jnp.zeros((), fetched.dtype))
    pixel_profiles = fetched.transpose(1, 0, 2, 3).reshape(NPIX, PROF)
    column_bin = angle_index[jnp.arange(NPIX, dtype=jnp.int32) % XTRACK]
    slant_path = 1.0 / jnp.cos(column_bin.astype(jnp.float32) * (max_zenith / (NANG - 1))) - 1.0
    model_terms = [jnp.dot(jacobian[m].T, pixel_profiles.T, preferred_element_type=jnp.float32) for m in range(3)]
    slant_row = slant_path[None, :]
    departure = observed.astype(jnp.float32) - (model_terms[0] + slant_row * model_terms[1] + slant_row * slant_row * model_terms[2])
    smooth_field = departure.reshape(CHAN, NLINES, XTRACK)
    along_rate = kappa[0][:, None, None]
    cross_rate = kappa[1][:, None, None]
    for sweep in range(3):
        padded = jnp.pad(smooth_field, ((0, 0), (1, 1), (1, 1)))
        along_sum = padded[:, 2:, 1:-1] + padded[:, :-2, 1:-1] - 2.0 * smooth_field
        cross_sum = padded[:, 1:-1, 2:] + padded[:, 1:-1, :-2] - 2.0 * smooth_field
        smooth_field = smooth_field + along_rate * along_sum + cross_rate * cross_sum
    smoothed = smooth_field.reshape(CHAN, NPIX).astype(jnp.bfloat16)
    return jnp.dot(factor, smoothed, preferred_element_type=jnp.float32)
```

```python
import math

import jax
import jax.numpy as jnp
from jax import lax
from jax.sharding import PartitionSpec as P

XTRACK = 128
NANG = 8
SWEEPS = 3

max_zenith = math.pi / 3.0


def edge_lines(block, width):
    count = lax.axis_size("swath")
    forward = [(i, i + 1) for i in range(count - 1)]
    backward = [(target, source) for source, target in forward]
    low = lax.ppermute(block[:, -width:], "swath", forward)
    high = lax.ppermute(block[:, :width], "swath", backward)
    return jnp.concatenate([low, block, high], axis=1)


def diffuse_once(extended, along_rate, cross_rate):
    center = extended[:, 1:-1]
    along_sum = extended[:, 2:] + extended[:, :-2] - 2.0 * center
    side_pad = jnp.pad(center, ((0, 0), (0, 0), (1, 1)))
    cross_sum = side_pad[:, :, 2:] + side_pad[:, :, :-2] - 2.0 * center
    return center + along_rate * along_sum + cross_rate * cross_sum


def on_device(grid_profiles, send_lists, counts, angle_index, jacobian, observed, kappa, factor):
    members = lax.axis_size("chan")
    member = lax.axis_index("chan")
    swaths = lax.axis_size("swath")
    swath = lax.axis_index("swath")
    slots = send_lists.shape[2]
    share = slots // members
    own_chan = observed.shape[0]
    pixel_count = observed.shape[1]
    line_count = pixel_count // XTRACK
    depth = grid_profiles.shape[1]

    rows = lax.dynamic_slice_in_dim(send_lists[0], member * share, share, axis=1)
    slot = member * share + jnp.arange(share, dtype=jnp.int32)
    live_slot = slot[None, :] < counts[0][:, None]
    zero_value = jnp.zeros((), grid_profiles.dtype)
    outgoing = jnp.where(live_slot[:, :, None], grid_profiles[rows], zero_value)
    incoming = lax.all_to_all(outgoing, "swath", split_axis=0, concat_axis=0, tiled=True)
    gathered = lax.all_gather(incoming, "chan", axis=0, tiled=False)
    pixel_profiles = gathered.transpose(1, 0, 2, 3).reshape(pixel_count, depth)
    whole_factor = lax.all_gather(factor, "chan", axis=0, tiled=True)

    model = jnp.einsum("mkc,pk->mcp", jacobian, pixel_profiles, preferred_element_type=jnp.float32)
    zenith = angle_index.astype(jnp.float32) * (max_zenith / (NANG - 1))
    slant_path = 1.0 / jnp.cos(zenith) - 1.0
    model = model.reshape(3, own_chan, line_count, XTRACK)
    departure = observed.astype(jnp.float32).reshape(own_chan, line_count, XTRACK) - (
        model[0] + slant_path * model[1] + slant_path * slant_path * model[2]
    )
    along_rate = kappa[0][:, None, None]
    cross_rate = kappa[1][:, None, None]
    field = edge_lines(departure, SWEEPS)
    line = swath * line_count - SWEEPS + jnp.arange(line_count + 2 * SWEEPS, dtype=jnp.int32)
    inside = (line >= 0) & (line < swaths * line_count)
    for sweep in range(SWEEPS):
        field = diffuse_once(field, along_rate, cross_rate)
        kept = inside[sweep + 1 : inside.shape[0] - sweep - 1]
        field = jnp.where(kept[None, :, None], field, 0.0)
    smoothed = field.reshape(own_chan, pixel_count).astype(jnp.bfloat16)
    every_channel = lax.all_to_all(smoothed, "chan", split_axis=1, concat_axis=0, tiled=True)
    weighted = jnp.dot(whole_factor, every_channel, preferred_element_type=jnp.float32)
    return lax.all_to_all(weighted, "chan", split_axis=0, concat_axis=1, tiled=True)


def solution(mesh):
    in_specs = (
        P("swath", None),
        P("swath", None, None),
        P("swath", None),
        P(),
        P(None, None, "chan"),
        P("chan", "swath"),
        P(None, "chan"),
        P("chan", None),
    )
    out_specs = P("chan", "swath")
    return jax.shard_map(
        on_device, mesh=mesh, in_specs=in_specs, out_specs=out_specs, check_vma=False
    )
```

```python
import functools
import math

import jax
import jax.numpy as jnp
from jax import lax
from jax.experimental import pallas as pl
from jax.experimental.pallas import tpu as pltpu
from jax.sharding import PartitionSpec as P

XTRACK = 128
NANG = 8
SWEEPS = 3
SIDE = 4
MEMBERS = SIDE * SIDE
SWATHS = 2 * MEMBERS
LINES = 32
DEPTH = 256
PADDED = 48
GROUP = 4
MESH = pl.DeviceIdType.MESH

max_zenith = math.pi / 3.0


def kernel(
    own_chan,
    outgoing,
    own_factor,
    jac,
    observed,
    slant,
    rates,
    out,
    profiles,
    factor,
    field,
    field_1,
    field_2,
    smoothed,
    every,
    product,
    arrived,
    slot_send,
    slot_recv,
    slot_local,
    ring_send,
    ring_recv,
    edge_send,
    edge_recv,
    there_send,
    there_recv,
    back_send,
    back_recv,
):
    swath = lax.axis_index("swath")
    chan = lax.axis_index("chan")
    x, y = chan // SIDE, chan % SIDE
    above = lax.rem(swath + 1, SWATHS)
    below = lax.rem(swath + SWATHS - 1, SWATHS)

    def member(route, first, second):
        dx, dy = (first, second) if route == 0 else (second, first)
        return lax.rem(x + dx + SIDE, SIDE) * SIDE + lax.rem(y + dy + SIDE, SIDE)

    def line_of(route, who):
        return lax.rem(who + SWATHS - swath, MEMBERS) + MEMBERS * route

    partners = [line_of(k, chan) for k in range(2)]

    barrier = pltpu.get_barrier_semaphore()
    for i in range(1, MEMBERS):
        other = lax.rem(chan + i, MEMBERS)
        pl.semaphore_signal(barrier, inc=1, device_id={"chan": other}, device_id_type=MESH)
    for other in (above, below):
        pl.semaphore_signal(barrier, inc=1, device_id={"swath": other}, device_id_type=MESH)
    for other in partners:

        @pl.when(other != swath)
        def _():
            pl.semaphore_signal(barrier, inc=1, device_id={"swath": other}, device_id_type=MESH)

    distinct = sum(jnp.where(other != swath, 1, 0) for other in partners)
    pl.semaphore_wait(barrier, MEMBERS + 1 + distinct)

    def slot_copy(k):
        return pltpu.make_async_remote_copy(
            src_ref=outgoing.at[k],
            dst_ref=profiles.at[swath],
            send_sem=slot_send.at[k],
            recv_sem=slot_recv.at[k],
            device_id={"swath": partners[k]},
            device_id_type=MESH,
        )

    def slot_kept(k):
        return pltpu.make_async_copy(outgoing.at[k], profiles.at[swath], slot_local.at[k])

    def slot_sent(k):
        half = swath // MEMBERS
        return pltpu.make_async_remote_copy(
            src_ref=outgoing.at[k],
            dst_ref=profiles.at[swath],
            send_sem=slot_send.at[k],
            recv_sem=slot_recv.at[half],
            device_id={"swath": partners[k]},
            device_id_type=MESH,
        )

    for k in range(2):

        @pl.when(partners[k] != swath)
        def _():
            slot_sent(k).start()

        @pl.when(partners[k] == swath)
        def _():
            slot_kept(k).start()

    def profile_piece(route, who):
        return profiles.at[line_of(route, who)]

    def profile_half(route, who, half):
        rows = XTRACK // 2
        return profiles.at[line_of(route, who), pl.ds(half * rows, rows)]

    def factor_piece(route, who):
        return factor.at[route, who]

    def factor_half(route, who, half):
        return factor.at[route, who, pl.ds(0, 32) if half == 0 else pl.ds(32, 16)]

    sent = []
    offsets = (0, -1, 1, 2)

    class Ring:
        def __init__(self, kind, route, piece, half):
            self.kind, self.route, self.piece, self.half = kind, route, piece, half
            self.copies = {}

        def send(self, key, number, source, target, to):
            at = (self.kind * 2 + self.route) * 20 + number
            copy = pltpu.make_async_remote_copy(
                src_ref=source,
                dst_ref=target,
                send_sem=ring_send.at[at],
                recv_sem=ring_recv.at[at],
                device_id={"chan": to},
                device_id_type=MESH,
            )
            copy.start()
            sent.append(copy)
            self.copies[key] = copy

        def whole(self, offset, source=None):
            who = member(self.route, offset, 0)
            target = self.piece(self.route, who)
            for way in range(2):
                to = member(self.route, 0, 1 - 2 * way)
                number = 4 + offsets.index(offset) * 2 + way
                self.send(("b", offset, way), number, target if source is None else source, target, to)

        def open(self, source=None):
            target = self.piece(self.route, chan)
            for way in range(2):
                to = member(self.route, 1 - 2 * way, 0)
                self.send(("a", way), way, target if source is None else source, target, to)
            self.whole(0, source)

        def relay(self):
            for way in range(2):
                self.copies["a", way].wait_recv()
                came = 2 * way - 1
                part = self.half(self.route, member(self.route, came, 0), way)
                self.send(("c", way), 2 + way, part, part, member(self.route, -came, 0))
                self.whole(came)

        def across(self):
            for way in range(2):
                self.copies["c", way].wait_recv()
            self.whole(2)

        def finish(self):
            for index, offset in enumerate(offsets):
                for way in range(2):
                    self.copies["b", offset, way].wait_recv()
                    came = 2 * way - 1
                    part = self.half(self.route, member(self.route, offset, came), way)
                    number = 12 + index * 2 + way
                    self.send(("d", offset, way), number, part, part, member(self.route, 0, -came))

        def close(self):
            for offset in offsets:
                for way in range(2):
                    self.copies["d", offset, way].wait_recv()

    profile_rings = [Ring(0, k, profile_piece, profile_half) for k in range(2)]
    factor_rings = [Ring(1, k, factor_piece, factor_half) for k in range(2)]

    for k, ring in enumerate(factor_rings):
        ring.open(own_factor.at[k])
    for k in range(2):
        factor[k, chan] = own_factor[k]
    for ring in factor_rings:
        ring.relay()
    for ring in factor_rings:
        ring.across()
    for k, ring in enumerate(profile_rings):

        @pl.when(partners[k] != swath)
        def _():
            slot_copy(k).wait_recv()

        @pl.when(partners[k] == swath)
        def _():
            slot_kept(k).wait()

        ring.open()
    for ring in factor_rings:
        ring.finish()
    for ring in profile_rings:
        ring.relay()
    for ring in profile_rings:
        ring.across()
    for ring in profile_rings:
        ring.finish()
    for ring in factor_rings:
        ring.close()
    for ring in profile_rings:
        ring.close()

    path = slant[...]
    path_2 = path * path

    def depart(group):
        start = group * GROUP
        rows = profiles[pl.ds(start, GROUP)].reshape(GROUP * XTRACK, DEPTH)
        model = lax.dot_general(
            jac[...], rows, (((1,), (1,)), ((), ())), preferred_element_type=jnp.float32
        )
        for i in range(GROUP):
            part = model[:, i * XTRACK : (i + 1) * XTRACK]
            columns = pl.ds(pl.multiple_of((start + i) * XTRACK, XTRACK), XTRACK)
            field[start + i + SWEEPS] = observed[:, columns].astype(jnp.float32) - (
                part[:PADDED]
                + path * part[PADDED : 2 * PADDED]
                + path_2 * part[2 * PADDED :]
            )

    depart(LINES // GROUP - 1)
    depart(0)
    depart(1)
    edges = []
    for way, (source, target, to) in enumerate(
        ((LINES, 0, above), (SWEEPS, LINES + SWEEPS, below))
    ):
        copy = pltpu.make_async_remote_copy(
            src_ref=field.at[pl.ds(source, SWEEPS)],
            dst_ref=field.at[pl.ds(target, SWEEPS)],
            send_sem=edge_send.at[way],
            recv_sem=edge_recv.at[way],
            device_id={"swath": to},
            device_id_type=MESH,
        )
        copy.start()
        edges.append(copy)
        sent.append(copy)

    @pl.loop(2, LINES // GROUP - 1)
    def _(group):
        depart(group)

    for copy in edges:
        copy.wait_recv()

    def clear(block, width):
        @pl.when(swath == 0)
        def _():
            block[pl.ds(0, width)] = jnp.zeros((width, PADDED, XTRACK), jnp.float32)

        @pl.when(swath == SWATHS - 1)
        def _():
            block[pl.ds(LINES + width, width)] = jnp.zeros((width, PADDED, XTRACK), jnp.float32)

    along_rate = rates[0]
    cross_rate = rates[1]
    column = lax.broadcasted_iota(jnp.int32, (PADDED, XTRACK), 1)

    def diffuse(block, at):
        center = block[at]
        along_sum = block[at + 1] + block[at - 1] - 2.0 * center
        left = jnp.where(column == 0, 0.0, pltpu.roll(center, 1, 1))
        right = jnp.where(column == XTRACK - 1, 0.0, pltpu.roll(center, XTRACK - 1, 1))
        cross_sum = right + left - 2.0 * center
        return center + along_rate * along_sum + cross_rate * cross_sum

    clear(field, 3)

    @pl.loop(0, (LINES + 4) // 2)
    def _(pair):
        for i in range(2):
            field_1[2 * pair + i] = diffuse(field, 2 * pair + i + 1)

    clear(field_1, 2)

    @pl.loop(0, (LINES + 2) // 2)
    def _(pair):
        for i in range(2):
            field_2[2 * pair + i] = diffuse(field_1, 2 * pair + i + 1)

    clear(field_2, 1)

    def there(who, into):
        return pltpu.make_async_remote_copy(
            src_ref=smoothed.at[pl.ds(2 * who, 2)],
            dst_ref=every.at[:, into],
            send_sem=there_send.at[who],
            recv_sem=there_recv.at[into],
            device_id={"chan": who},
            device_id_type=MESH,
        )

    def smooth_pair(i):
        who = lax.rem(chan + 1 + i, MEMBERS)
        for j in range(2):
            smoothed[2 * who + j] = diffuse(field_2, 2 * who + j + 1).astype(jnp.bfloat16)

    smooth_pair(0)

    @pl.loop(1, MEMBERS)
    def _(i):
        smooth_pair(i)
        there(lax.rem(chan + i, MEMBERS), chan).start()

    for j in range(2):
        every[j, chan] = smoothed[2 * chan + j]

    @pl.loop(1, MEMBERS)
    def _(i):
        who = lax.rem(chan + i, MEMBERS)
        there(who, who).wait_recv()

    pieces = [every[j].reshape(MEMBERS * PADDED, XTRACK) for j in range(2)]
    wide = jnp.concatenate(pieces, axis=1)
    half_depth = MEMBERS * PADDED // 2

    def weigh(group):
        rows = [
            factor[k, pl.ds(group * GROUP, GROUP)].reshape(GROUP * PADDED, half_depth)
            for k in range(2)
        ]
        block = jnp.dot(
            rows[0], wide[:half_depth], preferred_element_type=jnp.float32
        ) + jnp.dot(rows[1], wide[half_depth:], preferred_element_type=jnp.float32)
        for j in range(2):
            part = block[:, j * XTRACK : (j + 1) * XTRACK].astype(jnp.bfloat16)
            product[j, pl.ds(group * GROUP, GROUP)] = part.reshape(GROUP, PADDED, XTRACK)

    for group in range(MEMBERS // GROUP):
        weigh(group)

    def back(who, into):
        return pltpu.make_async_remote_copy(
            src_ref=product.at[:, who],
            dst_ref=arrived.at[pl.ds(2 * into, 2)],
            send_sem=back_send.at[who],
            recv_sem=back_recv.at[into],
            device_id={"chan": who},
            device_id_type=MESH,
        )

    @pl.loop(1, MEMBERS)
    def _(i):
        back(lax.rem(chan + i, MEMBERS), chan).start()

    for j in range(2):
        arrived[2 * chan + j] = product[j, chan]

    def settle(who):
        for j in range(2):
            at = 2 * who + j
            columns = pl.ds(pl.multiple_of(at * XTRACK, XTRACK), XTRACK)
            out[:, columns] = arrived[at].astype(jnp.float32)[:own_chan]

    settle(chan)

    @pl.loop(1, MEMBERS)
    def _(i):
        who = lax.rem(chan + i, MEMBERS)
        back(who, who).wait_recv()
        settle(who)

    for copy in sent:
        copy.wait_send()
    for k in range(2):

        @pl.when(partners[k] != swath)
        def _():
            slot_copy(k).wait_send()

    @pl.loop(1, MEMBERS)
    def _(i):
        who = lax.rem(chan + i, MEMBERS)
        there(who, chan).wait_send()
        back(who, chan).wait_send()


def on_device(grid_profiles, send_lists, counts, angle_index, jacobian, observed, kappa, factor):
    chan = lax.axis_index("chan")
    swath = lax.axis_index("swath")
    slots = send_lists.shape[2]
    own_chan = observed.shape[0]
    pixel_count = observed.shape[1]
    spare = PADDED - own_chan

    first = (chan - swath) % MEMBERS
    rows = send_lists[0].reshape(2, MEMBERS, slots)[:, first]
    live = counts[0].reshape(2, MEMBERS)[:, first]
    live_slot = jnp.arange(slots, dtype=jnp.int32)[None, :] < live[:, None]
    zero_value = jnp.zeros((), grid_profiles.dtype)
    outgoing = jnp.where(live_slot[:, :, None], grid_profiles[rows], zero_value)

    zenith = angle_index.astype(jnp.float32) * (max_zenith / (NANG - 1))
    slant_path = (1.0 / jnp.cos(zenith) - 1.0)[None, :]
    jac = jnp.pad(jacobian.transpose(0, 2, 1), ((0, 0), (0, spare), (0, 0)))
    jac = jac.reshape(3 * PADDED, DEPTH)
    padded = jnp.pad(observed, ((0, spare), (0, 0)))
    rates = jnp.broadcast_to(
        jnp.pad(kappa, ((0, 0), (0, spare)))[:, :, None], (2, PADDED, XTRACK)
    )
    own_factor = jnp.pad(
        factor.reshape(own_chan, MEMBERS, own_chan), ((0, spare), (0, 0), (0, spare))
    )
    half_depth = MEMBERS * PADDED // 2
    own_factor = own_factor.reshape(PADDED, 2, half_depth).transpose(1, 0, 2)

    vmem = pl.BlockSpec(memory_space=pltpu.VMEM)
    dma = pltpu.SemaphoreType.DMA
    return pl.pallas_call(
        functools.partial(kernel, own_chan),
        out_shape=jax.ShapeDtypeStruct((own_chan, pixel_count), jnp.float32),
        in_specs=[vmem] * 6,
        out_specs=vmem,
        scratch_shapes=[
            pltpu.VMEM((LINES, XTRACK, DEPTH), jnp.bfloat16),
            pltpu.VMEM((2, MEMBERS, PADDED, half_depth), jnp.bfloat16),
            pltpu.VMEM((LINES + 6, PADDED, XTRACK), jnp.float32),
            pltpu.VMEM((LINES + 4, PADDED, XTRACK), jnp.float32),
            pltpu.VMEM((LINES + 2, PADDED, XTRACK), jnp.float32),
            pltpu.VMEM((LINES, PADDED, XTRACK), jnp.bfloat16),
            pltpu.VMEM((2, MEMBERS, PADDED, XTRACK), jnp.bfloat16),
            pltpu.VMEM((2, MEMBERS, PADDED, XTRACK), jnp.bfloat16),
            pltpu.VMEM((LINES, PADDED, XTRACK), jnp.bfloat16),
            dma((2,)),
            dma((2,)),
            dma((2,)),
            dma((80,)),
            dma((80,)),
            dma((2,)),
            dma((2,)),
            dma((MEMBERS,)),
            dma((MEMBERS,)),
            dma((MEMBERS,)),
            dma((MEMBERS,)),
        ],
        compiler_params=pltpu.CompilerParams(collective_id=0, has_side_effects=True),
    )(outgoing, own_factor, jac, padded, slant_path, rates)


def solution(mesh):
    in_specs = (
        P("swath", None),
        P("swath", None, None),
        P("swath", None),
        P(),
        P(None, None, "chan"),
        P("chan", "swath"),
        P(None, "chan"),
        P("chan", None),
    )
    out_specs = P("chan", "swath")
    return jax.shard_map(
        on_device, mesh=mesh, in_specs=in_specs, out_specs=out_specs, check_vma=False
    )
```

```python
import functools
import math

import jax
import jax.numpy as jnp
from jax import lax
from jax.experimental import pallas as pl
from jax.experimental.pallas import tpu as pltpu
from jax.sharding import PartitionSpec as P

XTRACK = 128
NANG = 8
SWEEPS = 3
SIDE = 4
MEMBERS = SIDE * SIDE
SWATHS = 2 * MEMBERS
LINES = 32
DEPTH = 256
PADDED = 48
ROWS = 40
GROUP = 4
MESH = pl.DeviceIdType.MESH

max_zenith = math.pi / 3.0


def kernel(
    own_chan,
    grid,
    lists,
    counts,
    angle,
    jac_in,
    observed,
    kappa,
    factor_in,
    out,
    outgoing,
    own_factor,
    jac,
    weights,
    profiles,
    factor,
    field,
    field_1,
    field_2,
    smoothed,
    every,
    product,
    arrived,
    slot_send,
    slot_recv,
    slot_local,
    ring_send,
    ring_recv,
    edge_send,
    edge_recv,
    there_send,
    there_recv,
    back_send,
    back_recv,
):
    swath = lax.axis_index("swath")
    chan = lax.axis_index("chan")
    x, y = chan // SIDE, chan % SIDE
    above = lax.rem(swath + 1, SWATHS)
    below = lax.rem(swath + SWATHS - 1, SWATHS)

    def member(route, first, second):
        dx, dy = (first, second) if route == 0 else (second, first)
        return lax.rem(x + dx + SIDE, SIDE) * SIDE + lax.rem(y + dy + SIDE, SIDE)

    def line_of(route, who):
        return lax.rem(who + SWATHS - swath, MEMBERS) + MEMBERS * route

    partners = [line_of(k, chan) for k in range(2)]

    field[...] = jnp.zeros(field.shape, jnp.float32)
    barrier = pltpu.get_barrier_semaphore()
    for i in range(1, MEMBERS):
        other = lax.rem(chan + i, MEMBERS)
        pl.semaphore_signal(barrier, inc=1, device_id={"chan": other}, device_id_type=MESH)
    for other in (above, below):
        pl.semaphore_signal(barrier, inc=1, device_id={"swath": other}, device_id_type=MESH)
    for other in partners:

        @pl.when(other != swath)
        def _():
            pl.semaphore_signal(barrier, inc=1, device_id={"swath": other}, device_id_type=MESH)

    grid_rows = grid.shape[0]
    slot = lax.broadcasted_iota(jnp.int32, (1, XTRACK), 1)
    grid_row = lax.broadcasted_iota(jnp.int32, (grid_rows, XTRACK), 0)
    for k in range(2):
        picked = lists[pl.ds(partners[k], 1), :]
        picked = jnp.where(slot < counts[0, partners[k]], picked, -1)
        chosen = jnp.where(grid_row == picked, 1.0, 0.0).astype(jnp.bfloat16)
        outgoing[k] = lax.dot_general(
            chosen, grid[...], (((0,), (0,)), ((), ())), preferred_element_type=jnp.float32
        ).astype(jnp.bfloat16)

    channels = MEMBERS * own_chan
    place = lax.broadcasted_iota(jnp.int32, (1, MEMBERS * PADDED), 1)
    owner = sum(jnp.where(place >= m * PADDED, 1, 0) for m in range(1, MEMBERS))
    target = jnp.where(place - owner * PADDED < own_chan, place - owner * (PADDED - own_chan), -1)
    source_row = lax.broadcasted_iota(jnp.int32, (channels, MEMBERS * PADDED), 0)
    spread = jnp.where(source_row == target, 1.0, 0.0).astype(jnp.bfloat16)
    spaced = jnp.dot(factor_in[...], spread, preferred_element_type=jnp.float32)
    spaced = spaced.astype(jnp.bfloat16)
    half_depth = MEMBERS * PADDED // 2
    own_factor[...] = jnp.zeros(own_factor.shape, jnp.bfloat16)
    for k in range(2):
        own_factor[k, pl.ds(0, own_chan)] = spaced[:, k * half_depth : (k + 1) * half_depth]

    jac[...] = jnp.zeros(jac.shape, jnp.bfloat16)
    for m in range(3):
        jac[pl.ds(m * PADDED, own_chan)] = jac_in[m]

    smoothed[...] = jnp.zeros(smoothed.shape, jnp.bfloat16)

    distinct = sum(jnp.where(other != swath, 1, 0) for other in partners)
    pl.semaphore_wait(barrier, MEMBERS + 1 + distinct)

    def slot_copy(k):
        return pltpu.make_async_remote_copy(
            src_ref=outgoing.at[k],
            dst_ref=profiles.at[swath],
            send_sem=slot_send.at[k],
            recv_sem=slot_recv.at[k],
            device_id={"swath": partners[k]},
            device_id_type=MESH,
        )

    def slot_kept(k):
        return pltpu.make_async_copy(outgoing.at[k], profiles.at[swath], slot_local.at[k])

    def slot_sent(k):
        half = swath // MEMBERS
        return pltpu.make_async_remote_copy(
            src_ref=outgoing.at[k],
            dst_ref=profiles.at[swath],
            send_sem=slot_send.at[k],
            recv_sem=slot_recv.at[half],
            device_id={"swath": partners[k]},
            device_id_type=MESH,
        )

    for k in range(2):

        @pl.when(partners[k] != swath)
        def _():
            slot_sent(k).start()

        @pl.when(partners[k] == swath)
        def _():
            slot_kept(k).start()

    def profile_piece(route, who):
        return profiles.at[line_of(route, who)]

    def profile_half(route, who, half):
        rows = XTRACK // 2
        return profiles.at[line_of(route, who), pl.ds(half * rows, rows)]

    def factor_piece(route, who):
        return factor.at[route, who]

    def factor_half(route, who, half):
        return factor.at[route, who, pl.ds(0, 32) if half == 0 else pl.ds(32, 16)]

    sent = []
    offsets = (0, -1, 1, 2)

    class Ring:
        def __init__(self, kind, route, piece, half):
            self.kind, self.route, self.piece, self.half = kind, route, piece, half
            self.copies = {}

        def send(self, key, number, source, target, to):
            at = (self.kind * 2 + self.route) * 20 + number
            copy = pltpu.make_async_remote_copy(
                src_ref=source,
                dst_ref=target,
                send_sem=ring_send.at[at],
                recv_sem=ring_recv.at[at],
                device_id={"chan": to},
                device_id_type=MESH,
            )
            copy.start()
            sent.append(copy)
            self.copies[key] = copy

        def whole(self, offset, source=None):
            who = member(self.route, offset, 0)
            target = self.piece(self.route, who)
            for way in range(2):
                to = member(self.route, 0, 1 - 2 * way)
                number = 4 + offsets.index(offset) * 2 + way
                self.send(("b", offset, way), number, target if source is None else source, target, to)

        def open(self, source=None):
            target = self.piece(self.route, chan)
            for way in range(2):
                to = member(self.route, 1 - 2 * way, 0)
                self.send(("a", way), way, target if source is None else source, target, to)
            self.whole(0, source)

        def relay(self):
            for way in range(2):
                self.copies["a", way].wait_recv()
                came = 2 * way - 1
                part = self.half(self.route, member(self.route, came, 0), way)
                self.send(("c", way), 2 + way, part, part, member(self.route, -came, 0))
                self.whole(came)

        def across(self):
            for way in range(2):
                self.copies["c", way].wait_recv()
            self.whole(2)

        def finish(self):
            for index, offset in enumerate(offsets):
                for way in range(2):
                    self.copies["b", offset, way].wait_recv()
                    came = 2 * way - 1
                    part = self.half(self.route, member(self.route, offset, came), way)
                    number = 12 + index * 2 + way
                    self.send(("d", offset, way), number, part, part, member(self.route, 0, -came))

        def close(self):
            for offset in offsets:
                for way in range(2):
                    self.copies["d", offset, way].wait_recv()

    profile_rings = [Ring(0, k, profile_piece, profile_half) for k in range(2)]
    factor_rings = [Ring(1, k, factor_piece, factor_half) for k in range(2)]

    for k, ring in enumerate(factor_rings):
        ring.open(own_factor.at[k])
    for k in range(2):
        factor[k, chan] = own_factor[k]
    for ring in factor_rings:
        ring.relay()
    for ring in factor_rings:
        ring.across()
    for k, ring in enumerate(profile_rings):

        @pl.when(partners[k] != swath)
        def _():
            slot_copy(k).wait_recv()

        @pl.when(partners[k] == swath)
        def _():
            slot_kept(k).wait()

        ring.open()
    for ring in factor_rings:
        ring.finish()
    for ring in profile_rings:
        ring.relay()
    for ring in profile_rings:
        ring.across()
    for ring in profile_rings:
        ring.finish()
    zenith = angle[...].astype(jnp.float32) * (max_zenith / (NANG - 1))
    path = 1.0 / jnp.cos(zenith) - 1.0
    path_2 = path * path

    def depart(route, first, second):
        line = line_of(route, member(route, first, second))
        model = lax.dot_general(
            jac[...], profiles[line], (((1,), (1,)), ((), ())), preferred_element_type=jnp.float32
        )
        columns = pl.ds(pl.multiple_of(line * XTRACK, XTRACK), XTRACK)
        value = (
            model[:PADDED]
            + path * model[PADDED : 2 * PADDED]
            + path_2 * model[2 * PADDED :]
        )
        field[line + SWEEPS, pl.ds(0, own_chan)] = (
            observed[:, columns].astype(jnp.float32) - value[:own_chan]
        )

    @pl.loop(0, 3)
    def _(i):
        for route in range(2):
            for first in offsets:
                depart(route, first, i - 1)

    for ring in factor_rings:
        ring.close()
    for ring in profile_rings:
        ring.close()
    for route in range(2):
        for first in offsets:
            depart(route, first, 2)

    column = lax.broadcasted_iota(jnp.int32, (ROWS, XTRACK), 1)
    on_diagonal = lax.broadcasted_iota(jnp.int32, (ROWS, own_chan), 0) == (
        lax.broadcasted_iota(jnp.int32, (ROWS, own_chan), 1)
    )
    spread_rates = [
        jnp.broadcast_to(
            jnp.sum(jnp.where(on_diagonal, kappa[pl.ds(k, 1), :], 0.0), axis=1, keepdims=True),
            (ROWS, XTRACK),
        )
        for k in range(2)
    ]
    weights[0] = 1.0 - 2.0 * (spread_rates[0] + spread_rates[1])
    weights[1] = spread_rates[0]
    weights[2] = jnp.where(column == 0, 0.0, spread_rates[1])
    weights[3] = jnp.where(column == XTRACK - 1, 0.0, spread_rates[1])

    edges = []
    for way, (source, target, to) in enumerate(
        ((LINES, 0, above), (SWEEPS, LINES + SWEEPS, below))
    ):
        copy = pltpu.make_async_remote_copy(
            src_ref=field.at[pl.ds(source, SWEEPS)],
            dst_ref=field.at[pl.ds(target, SWEEPS)],
            send_sem=edge_send.at[way],
            recv_sem=edge_recv.at[way],
            device_id={"swath": to},
            device_id_type=MESH,
        )
        copy.start()
        edges.append(copy)
        sent.append(copy)

    for copy in edges:
        copy.wait_recv()

    def clear(block, width):
        @pl.when(swath == 0)
        def _():
            block[pl.ds(0, width)] = jnp.zeros((width, ROWS, XTRACK), jnp.float32)

        @pl.when(swath == SWATHS - 1)
        def _():
            block[pl.ds(LINES + width, width)] = jnp.zeros((width, ROWS, XTRACK), jnp.float32)

    weight = [weights[k] for k in range(4)]

    def diffuse(block, at):
        center = block[at]
        left = pltpu.roll(center, 1, 1)
        right = pltpu.roll(center, XTRACK - 1, 1)
        return (
            weight[0] * center
            + weight[1] * (block[at + 1] + block[at - 1])
            + (weight[2] * left + weight[3] * right)
        )

    def sweep(source, target, count, step):
        @pl.loop(0, count // step)
        def _(turn):
            for i in range(step):
                target[step * turn + i] = diffuse(source, step * turn + i + 1)

        for at in range(count - count % step, count):
            target[at] = diffuse(source, at + 1)

    clear(field, 3)

    sweep(field, field_1, LINES + 4, 6)
    clear(field_1, 2)

    sweep(field_1, field_2, LINES + 2, 6)
    clear(field_2, 1)

    def there(who, into):
        return pltpu.make_async_remote_copy(
            src_ref=smoothed.at[pl.ds(2 * who, 2)],
            dst_ref=every.at[:, into],
            send_sem=there_send.at[who],
            recv_sem=there_recv.at[into],
            device_id={"chan": who},
            device_id_type=MESH,
        )

    def smooth_pair(i):
        who = lax.rem(chan + 1 + i, MEMBERS)
        for j in range(2):
            value = diffuse(field_2, 2 * who + j + 1).astype(jnp.bfloat16)
            smoothed[2 * who + j, pl.ds(0, ROWS)] = value

    smooth_pair(0)

    @pl.loop(1, MEMBERS)
    def _(i):
        smooth_pair(i)
        there(lax.rem(chan + i, MEMBERS), chan).start()

    for j in range(2):
        every[j, chan] = smoothed[2 * chan + j]

    @pl.loop(1, MEMBERS)
    def _(i):
        who = lax.rem(chan + i, MEMBERS)
        there(who, who).wait_recv()

    pieces = [every[j].reshape(MEMBERS * PADDED, XTRACK) for j in range(2)]
    wide = jnp.concatenate(pieces, axis=1)

    def weigh(group):
        rows = [
            factor[k, pl.ds(group * GROUP, GROUP)].reshape(GROUP * PADDED, half_depth)
            for k in range(2)
        ]
        block = jnp.dot(
            rows[0], wide[:half_depth], preferred_element_type=jnp.float32
        ) + jnp.dot(rows[1], wide[half_depth:], preferred_element_type=jnp.float32)
        for j in range(2):
            part = block[:, j * XTRACK : (j + 1) * XTRACK].astype(jnp.bfloat16)
            product[j, pl.ds(group * GROUP, GROUP)] = part.reshape(GROUP, PADDED, XTRACK)

    for group in range(MEMBERS // GROUP):
        weigh(group)

    def back(who, into):
        return pltpu.make_async_remote_copy(
            src_ref=product.at[:, who],
            dst_ref=arrived.at[pl.ds(2 * into, 2)],
            send_sem=back_send.at[who],
            recv_sem=back_recv.at[into],
            device_id={"chan": who},
            device_id_type=MESH,
        )

    @pl.loop(1, MEMBERS)
    def _(i):
        back(lax.rem(chan + i, MEMBERS), chan).start()

    for j in range(2):
        arrived[2 * chan + j] = product[j, chan]

    def settle(who):
        for j in range(2):
            at = 2 * who + j
            columns = pl.ds(pl.multiple_of(at * XTRACK, XTRACK), XTRACK)
            out[:, columns] = arrived[at, pl.ds(0, own_chan)]

    settle(chan)

    @pl.loop(1, MEMBERS)
    def _(i):
        who = lax.rem(chan + i, MEMBERS)
        back(who, who).wait_recv()
        settle(who)

    for copy in sent:
        copy.wait_send()
    for k in range(2):

        @pl.when(partners[k] != swath)
        def _():
            slot_copy(k).wait_send()

    @pl.loop(1, MEMBERS)
    def _(i):
        who = lax.rem(chan + i, MEMBERS)
        there(who, chan).wait_send()
        back(who, chan).wait_send()


def on_device(grid_profiles, send_lists, counts, angle_index, jacobian, observed, kappa, factor):
    own_chan = observed.shape[0]
    pixel_count = observed.shape[1]
    half_depth = MEMBERS * PADDED // 2
    vmem = pl.BlockSpec(memory_space=pltpu.VMEM)
    dma = pltpu.SemaphoreType.DMA
    weighted = pl.pallas_call(
        functools.partial(kernel, own_chan),
        out_shape=jax.ShapeDtypeStruct((own_chan, pixel_count), jnp.bfloat16),
        in_specs=[vmem, vmem, pl.BlockSpec(memory_space=pltpu.SMEM)] + [vmem] * 5,
        out_specs=vmem,
        scratch_shapes=[
            pltpu.VMEM((2, XTRACK, DEPTH), jnp.bfloat16),
            pltpu.VMEM((2, PADDED, half_depth), jnp.bfloat16),
            pltpu.VMEM((3 * PADDED, DEPTH), jnp.bfloat16),
            pltpu.VMEM((4, ROWS, XTRACK), jnp.float32),
            pltpu.VMEM((LINES, XTRACK, DEPTH), jnp.bfloat16),
            pltpu.VMEM((2, MEMBERS, PADDED, half_depth), jnp.bfloat16),
            pltpu.VMEM((LINES + 6, ROWS, XTRACK), jnp.float32),
            pltpu.VMEM((LINES + 4, ROWS, XTRACK), jnp.float32),
            pltpu.VMEM((LINES + 2, ROWS, XTRACK), jnp.float32),
            pltpu.VMEM((LINES, PADDED, XTRACK), jnp.bfloat16),
            pltpu.VMEM((2, MEMBERS, PADDED, XTRACK), jnp.bfloat16),
            pltpu.VMEM((2, MEMBERS, PADDED, XTRACK), jnp.bfloat16),
            pltpu.VMEM((LINES, PADDED, XTRACK), jnp.bfloat16),
            dma((2,)),
            dma((2,)),
            dma((2,)),
            dma((80,)),
            dma((80,)),
            dma((2,)),
            dma((2,)),
            dma((MEMBERS,)),
            dma((MEMBERS,)),
            dma((MEMBERS,)),
            dma((MEMBERS,)),
        ],
        compiler_params=pltpu.CompilerParams(collective_id=0, has_side_effects=True),
    )(
        grid_profiles,
        send_lists[0],
        counts,
        angle_index[None, :],
        jacobian.transpose(0, 2, 1),
        observed,
        kappa,
        factor,
    )
    return weighted.astype(jnp.float32)


def solution(mesh):
    in_specs = (
        P("swath", None),
        P("swath", None, None),
        P("swath", None),
        P(),
        P(None, None, "chan"),
        P("chan", "swath"),
        P(None, "chan"),
        P("chan", None),
    )
    out_specs = P("chan", "swath")
    return jax.shard_map(
        on_device, mesh=mesh, in_specs=in_specs, out_specs=out_specs, check_vma=False
    )
```

```python
import functools
import math

import jax
import jax.numpy as jnp
from jax import lax
from jax.experimental import pallas as pl
from jax.experimental.pallas import tpu as pltpu
from jax.sharding import PartitionSpec as P

XTRACK = 128
NANG = 8
SWEEPS = 3
SIDE = 4
MEMBERS = SIDE * SIDE
SWATHS = 2 * MEMBERS
LINES = 32
DEPTH = 256
PADDED = 48
ROWS = 40
GROUP = 4
MESH = pl.DeviceIdType.MESH

max_zenith = math.pi / 3.0


def kernel(
    own_chan,
    grid_in,
    lists,
    counts,
    angle,
    jac_held,
    observed_in,
    kappa,
    factor_held,
    result,
    grid,
    jac_in,
    observed,
    factor_in,
    out,
    outgoing,
    own_factor,
    jac,
    weights,
    profiles,
    factor,
    field,
    field_1,
    field_2,
    smoothed,
    every,
    product,
    arrived,
    slot_send,
    slot_recv,
    slot_local,
    ring_send,
    ring_recv,
    edge_send,
    edge_recv,
    there_send,
    there_recv,
    back_send,
    back_recv,
    load_sem,
    store_sem,
):
    swath = lax.axis_index("swath")
    chan = lax.axis_index("chan")
    x, y = chan // SIDE, chan % SIDE
    above = lax.rem(swath + 1, SWATHS)
    below = lax.rem(swath + SWATHS - 1, SWATHS)

    def member(route, first, second):
        dx, dy = (first, second) if route == 0 else (second, first)
        return lax.rem(x + dx + SIDE, SIDE) * SIDE + lax.rem(y + dy + SIDE, SIDE)

    def line_of(route, who):
        return lax.rem(who + SWATHS - swath, MEMBERS) + MEMBERS * route

    partners = [line_of(k, chan) for k in range(2)]

    field[...] = jnp.zeros(field.shape, jnp.float32)
    barrier = pltpu.get_barrier_semaphore()
    for i in range(1, MEMBERS):
        other = lax.rem(chan + i, MEMBERS)
        pl.semaphore_signal(barrier, inc=1, device_id={"chan": other}, device_id_type=MESH)
    for other in (above, below):
        pl.semaphore_signal(barrier, inc=1, device_id={"swath": other}, device_id_type=MESH)
    for other in partners:

        @pl.when(other != swath)
        def _():
            pl.semaphore_signal(barrier, inc=1, device_id={"swath": other}, device_id_type=MESH)

    loads = [
        pltpu.make_async_copy(held, block, load_sem.at[i])
        for i, (held, block) in enumerate(
            ((grid_in, grid), (factor_held, factor_in), (jac_held, jac_in), (observed_in, observed))
        )
    ]
    for load in loads:
        load.start()

    loads[0].wait()
    grid_rows = grid.shape[0]
    slot = lax.broadcasted_iota(jnp.int32, (1, XTRACK), 1)
    grid_row = lax.broadcasted_iota(jnp.int32, (grid_rows, XTRACK), 0)
    for k in range(2):
        picked = lists[pl.ds(partners[k], 1), :]
        picked = jnp.where(slot < counts[0, partners[k]], picked, -1)
        chosen = jnp.where(grid_row == picked, 1.0, 0.0).astype(jnp.bfloat16)
        outgoing[k] = lax.dot_general(
            chosen, grid[...], (((0,), (0,)), ((), ())), preferred_element_type=jnp.float32
        ).astype(jnp.bfloat16)

    channels = MEMBERS * own_chan
    place = lax.broadcasted_iota(jnp.int32, (1, MEMBERS * PADDED), 1)
    owner = sum(jnp.where(place >= m * PADDED, 1, 0) for m in range(1, MEMBERS))
    target = jnp.where(place - owner * PADDED < own_chan, place - owner * (PADDED - own_chan), -1)
    source_row = lax.broadcasted_iota(jnp.int32, (channels, MEMBERS * PADDED), 0)
    spread = jnp.where(source_row == target, 1.0, 0.0).astype(jnp.bfloat16)
    loads[1].wait()
    spaced = jnp.dot(factor_in[...], spread, preferred_element_type=jnp.float32)
    spaced = spaced.astype(jnp.bfloat16)
    half_depth = MEMBERS * PADDED // 2
    own_factor[...] = jnp.zeros(own_factor.shape, jnp.bfloat16)
    for k in range(2):
        own_factor[k, pl.ds(0, own_chan)] = spaced[:, k * half_depth : (k + 1) * half_depth]

    loads[2].wait()
    loads[3].wait()
    jac[...] = jnp.zeros(jac.shape, jnp.bfloat16)
    for m in range(3):
        jac[pl.ds(m * PADDED, own_chan)] = jac_in[m]

    smoothed[...] = jnp.zeros(smoothed.shape, jnp.bfloat16)

    distinct = sum(jnp.where(other != swath, 1, 0) for other in partners)
    pl.semaphore_wait(barrier, MEMBERS + 1 + distinct)

    def slot_copy(k):
        return pltpu.make_async_remote_copy(
            src_ref=outgoing.at[k],
            dst_ref=profiles.at[swath],
            send_sem=slot_send.at[k],
            recv_sem=slot_recv.at[k],
            device_id={"swath": partners[k]},
            device_id_type=MESH,
        )

    def slot_kept(k):
        return pltpu.make_async_copy(outgoing.at[k], profiles.at[swath], slot_local.at[k])

    def slot_sent(k):
        half = swath // MEMBERS
        return pltpu.make_async_remote_copy(
            src_ref=outgoing.at[k],
            dst_ref=profiles.at[swath],
            send_sem=slot_send.at[k],
            recv_sem=slot_recv.at[half],
            device_id={"swath": partners[k]},
            device_id_type=MESH,
        )

    for k in range(2):

        @pl.when(partners[k] != swath)
        def _():
            slot_sent(k).start()

        @pl.when(partners[k] == swath)
        def _():
            slot_kept(k).start()

    def profile_piece(route, who):
        return profiles.at[line_of(route, who)]

    def profile_half(route, who, half):
        rows = XTRACK // 2
        return profiles.at[line_of(route, who), pl.ds(half * rows, rows)]

    def factor_piece(route, who):
        return factor.at[route, who]

    def factor_half(route, who, half):
        return factor.at[route, who, pl.ds(0, 32) if half == 0 else pl.ds(32, 16)]

    sent = []
    offsets = (0, -1, 1, 2)

    class Ring:
        def __init__(self, kind, route, piece, half):
            self.kind, self.route, self.piece, self.half = kind, route, piece, half
            self.copies = {}

        def send(self, key, number, source, target, to):
            at = (self.kind * 2 + self.route) * 20 + number
            copy = pltpu.make_async_remote_copy(
                src_ref=source,
                dst_ref=target,
                send_sem=ring_send.at[at],
                recv_sem=ring_recv.at[at],
                device_id={"chan": to},
                device_id_type=MESH,
            )
            copy.start()
            sent.append(copy)
            self.copies[key] = copy

        def whole(self, offset, source=None):
            who = member(self.route, offset, 0)
            target = self.piece(self.route, who)
            for way in range(2):
                to = member(self.route, 0, 1 - 2 * way)
                number = 4 + offsets.index(offset) * 2 + way
                self.send(("b", offset, way), number, target if source is None else source, target, to)

        def open(self, source=None):
            target = self.piece(self.route, chan)
            for way in range(2):
                to = member(self.route, 1 - 2 * way, 0)
                self.send(("a", way), way, target if source is None else source, target, to)
            self.whole(0, source)

        def relay(self):
            for way in range(2):
                self.copies["a", way].wait_recv()
                came = 2 * way - 1
                part = self.half(self.route, member(self.route, came, 0), way)
                self.send(("c", way), 2 + way, part, part, member(self.route, -came, 0))
                self.whole(came)

        def across(self):
            for way in range(2):
                self.copies["c", way].wait_recv()
            self.whole(2)

        def finish(self):
            for index, offset in enumerate(offsets):
                for way in range(2):
                    self.copies["b", offset, way].wait_recv()
                    came = 2 * way - 1
                    part = self.half(self.route, member(self.route, offset, came), way)
                    number = 12 + index * 2 + way
                    self.send(("d", offset, way), number, part, part, member(self.route, 0, -came))

        def close(self):
            for offset in offsets:
                for way in range(2):
                    self.copies["d", offset, way].wait_recv()

    profile_rings = [Ring(0, k, profile_piece, profile_half) for k in range(2)]
    factor_rings = [Ring(1, k, factor_piece, factor_half) for k in range(2)]

    for k, ring in enumerate(factor_rings):
        ring.open(own_factor.at[k])
    for k in range(2):
        factor[k, chan] = own_factor[k]
    for ring in factor_rings:
        ring.relay()
    for ring in factor_rings:
        ring.across()
    for k, ring in enumerate(profile_rings):

        @pl.when(partners[k] != swath)
        def _():
            slot_copy(k).wait_recv()

        @pl.when(partners[k] == swath)
        def _():
            slot_kept(k).wait()

        ring.open()
    for ring in factor_rings:
        ring.finish()
    for ring in profile_rings:
        ring.relay()
    for ring in profile_rings:
        ring.across()
    for ring in profile_rings:
        ring.finish()
    zenith = angle[...].astype(jnp.float32) * (max_zenith / (NANG - 1))
    path = 1.0 / jnp.cos(zenith) - 1.0
    path_2 = path * path

    def depart(route, first, second):
        line = line_of(route, member(route, first, second))
        model = lax.dot_general(
            jac[...], profiles[line], (((1,), (1,)), ((), ())), preferred_element_type=jnp.float32
        )
        columns = pl.ds(pl.multiple_of(line * XTRACK, XTRACK), XTRACK)
        value = (
            model[:PADDED]
            + path * model[PADDED : 2 * PADDED]
            + path_2 * model[2 * PADDED :]
        )
        field[line + SWEEPS, pl.ds(0, own_chan)] = (
            observed[:, columns].astype(jnp.float32) - value[:own_chan]
        )

    @pl.loop(0, 3)
    def _(i):
        for route in range(2):
            for first in offsets:
                depart(route, first, i - 1)

    for ring in factor_rings:
        ring.close()
    for ring in profile_rings:
        ring.close()
    for route in range(2):
        for first in offsets:
            depart(route, first, 2)

    column = lax.broadcasted_iota(jnp.int32, (ROWS, XTRACK), 1)
    on_diagonal = lax.broadcasted_iota(jnp.int32, (ROWS, own_chan), 0) == (
        lax.broadcasted_iota(jnp.int32, (ROWS, own_chan), 1)
    )
    spread_rates = [
        jnp.broadcast_to(
            jnp.sum(jnp.where(on_diagonal, kappa[pl.ds(k, 1), :], 0.0), axis=1, keepdims=True),
            (ROWS, XTRACK),
        )
        for k in range(2)
    ]
    weights[0] = 1.0 - 2.0 * (spread_rates[0] + spread_rates[1])
    weights[1] = spread_rates[0]
    weights[2] = jnp.where(column == 0, 0.0, spread_rates[1])
    weights[3] = jnp.where(column == XTRACK - 1, 0.0, spread_rates[1])

    edges = []
    for way, (source, target, to) in enumerate(
        ((LINES, 0, above), (SWEEPS, LINES + SWEEPS, below))
    ):
        copy = pltpu.make_async_remote_copy(
            src_ref=field.at[pl.ds(source, SWEEPS)],
            dst_ref=field.at[pl.ds(target, SWEEPS)],
            send_sem=edge_send.at[way],
            recv_sem=edge_recv.at[way],
            device_id={"swath": to},
            device_id_type=MESH,
        )
        copy.start()
        edges.append(copy)
        sent.append(copy)

    def clear(block, width):
        @pl.when(swath == 0)
        def _():
            block[pl.ds(0, width)] = jnp.zeros((width, ROWS, XTRACK), jnp.float32)

        @pl.when(swath == SWATHS - 1)
        def _():
            block[pl.ds(LINES + width, width)] = jnp.zeros((width, ROWS, XTRACK), jnp.float32)

    weight = [weights[k] for k in range(4)]

    def diffuse(block, at):
        center = block[at]
        left = pltpu.roll(center, 1, 1)
        right = pltpu.roll(center, XTRACK - 1, 1)
        return (
            weight[0] * center
            + weight[1] * (block[at + 1] + block[at - 1])
            + (weight[2] * left + weight[3] * right)
        )

    def sweep(source, target, start, count, step):
        @pl.loop(0, count // step)
        def _(turn):
            for i in range(step):
                at = start + step * turn + i
                target[at] = diffuse(source, at + 1)

        for at in range(start + count - count % step, start + count):
            target[at] = diffuse(source, at + 1)

    def there(who, into):
        return pltpu.make_async_remote_copy(
            src_ref=smoothed.at[pl.ds(2 * who, 2)],
            dst_ref=every.at[:, into],
            send_sem=there_send.at[who],
            recv_sem=there_recv.at[into],
            device_id={"chan": who},
            device_id_type=MESH,
        )

    def smooth_pair(who):
        for j in range(2):
            value = diffuse(field_2, 2 * who + j + 1).astype(jnp.bfloat16)
            smoothed[2 * who + j, pl.ds(0, ROWS)] = value

    def send_pair(who):
        @pl.when(who != chan)
        def _():
            there(who, chan).start()

    inner = MEMBERS - 4

    def inner_member(i):
        return 2 + lax.rem(chan + i, inner)

    sweep(field, field_1, SWEEPS, LINES - 2, 6)
    sweep(field_1, field_2, SWEEPS, LINES - 4, 7)
    smooth_pair(inner_member(0))

    @pl.loop(1, inner)
    def _(i):
        smooth_pair(inner_member(i))
        send_pair(inner_member(i - 1))

    for copy in edges:
        copy.wait_recv()
    clear(field, 3)
    for start in (0, LINES + 1):
        sweep(field, field_1, start, 3, 3)
    clear(field_1, 2)
    for start in (0, LINES - 1):
        sweep(field_1, field_2, start, 3, 3)
    clear(field_2, 1)
    send_pair(inner_member(inner - 1))
    outer = (0, MEMBERS - 1, 1, MEMBERS - 2)
    for who in outer:
        smooth_pair(who)
    for who in outer:
        send_pair(who)

    for j in range(2):
        every[j, chan] = smoothed[2 * chan + j]

    @pl.loop(1, MEMBERS)
    def _(i):
        who = lax.rem(chan + i, MEMBERS)
        there(who, who).wait_recv()

    pieces = [every[j].reshape(MEMBERS * PADDED, XTRACK) for j in range(2)]
    wide = jnp.concatenate(pieces, axis=1)

    def weigh(group):
        rows = [
            factor[k, pl.ds(group * GROUP, GROUP)].reshape(GROUP * PADDED, half_depth)
            for k in range(2)
        ]
        block = jnp.dot(
            rows[0], wide[:half_depth], preferred_element_type=jnp.float32
        ) + jnp.dot(rows[1], wide[half_depth:], preferred_element_type=jnp.float32)
        for j in range(2):
            part = block[:, j * XTRACK : (j + 1) * XTRACK].astype(jnp.bfloat16)
            product[j, pl.ds(group * GROUP, GROUP)] = part.reshape(GROUP, PADDED, XTRACK)

    def back(who, into):
        return pltpu.make_async_remote_copy(
            src_ref=product.at[:, who],
            dst_ref=arrived.at[pl.ds(2 * into, 2)],
            send_sem=back_send.at[who],
            recv_sem=back_recv.at[into],
            device_id={"chan": who},
            device_id_type=MESH,
        )

    groups = MEMBERS // GROUP

    def group_at(i):
        return lax.rem(chan // GROUP + 1 + i, groups)

    def send_group(group):
        for i in range(GROUP):
            who = group * GROUP + lax.rem(chan + i, GROUP)

            @pl.when(who != chan)
            def _():
                back(who, chan).start()

    for i in range(groups):
        weigh(group_at(i))
        if i > 0:
            send_group(group_at(i - 1))
    send_group(group_at(groups - 1))

    for j in range(2):
        arrived[2 * chan + j] = product[j, chan]

    def settle(who):
        for j in range(2):
            at = 2 * who + j
            columns = pl.ds(pl.multiple_of(at * XTRACK, XTRACK), XTRACK)
            out[:, columns] = arrived[at, pl.ds(0, own_chan)]

    def store(who):
        columns = pl.ds(pl.multiple_of(2 * who * XTRACK, 2 * XTRACK), 2 * XTRACK)
        return pltpu.make_async_copy(
            out.at[:, columns], result.at[:, columns], store_sem.at[who]
        )

    settle(chan)

    @pl.loop(1, MEMBERS)
    def _(i):
        who = lax.rem(chan + i, MEMBERS)
        back(who, who).wait_recv()
        settle(who)
        store(lax.rem(chan + i - 1, MEMBERS)).start()

    for copy in sent:
        copy.wait_send()
    for k in range(2):

        @pl.when(partners[k] != swath)
        def _():
            slot_copy(k).wait_send()

    store(lax.rem(chan + MEMBERS - 1, MEMBERS)).start()

    @pl.loop(1, MEMBERS)
    def _(i):
        who = lax.rem(chan + i, MEMBERS)
        there(who, chan).wait_send()
        back(who, chan).wait_send()

    @pl.loop(0, MEMBERS)
    def _(who):
        store(who).wait()


def on_device(grid_profiles, send_lists, counts, angle_index, jacobian, observed, kappa, factor):
    own_chan = observed.shape[0]
    pixel_count = observed.shape[1]
    half_depth = MEMBERS * PADDED // 2
    vmem = pl.BlockSpec(memory_space=pltpu.VMEM)
    held = pl.BlockSpec(memory_space=pl.ANY)
    dma = pltpu.SemaphoreType.DMA
    weighted = pl.pallas_call(
        functools.partial(kernel, own_chan),
        out_shape=jax.ShapeDtypeStruct((own_chan, pixel_count), jnp.bfloat16),
        in_specs=[held, vmem, pl.BlockSpec(memory_space=pltpu.SMEM), vmem, held, held, vmem, held],
        out_specs=held,
        scratch_shapes=[
            pltpu.VMEM(grid_profiles.shape, jnp.bfloat16),
            pltpu.VMEM((3, own_chan, DEPTH), jnp.bfloat16),
            pltpu.VMEM(observed.shape, jnp.bfloat16),
            pltpu.VMEM(factor.shape, jnp.bfloat16),
            pltpu.VMEM(observed.shape, jnp.bfloat16),
            pltpu.VMEM((2, XTRACK, DEPTH), jnp.bfloat16),
            pltpu.VMEM((2, PADDED, half_depth), jnp.bfloat16),
            pltpu.VMEM((3 * PADDED, DEPTH), jnp.bfloat16),
            pltpu.VMEM((4, ROWS, XTRACK), jnp.float32),
            pltpu.VMEM((LINES, XTRACK, DEPTH), jnp.bfloat16),
            pltpu.VMEM((2, MEMBERS, PADDED, half_depth), jnp.bfloat16),
            pltpu.VMEM((LINES + 6, ROWS, XTRACK), jnp.float32),
            pltpu.VMEM((LINES + 4, ROWS, XTRACK), jnp.float32),
            pltpu.VMEM((LINES + 2, ROWS, XTRACK), jnp.float32),
            pltpu.VMEM((LINES, PADDED, XTRACK), jnp.bfloat16),
            pltpu.VMEM((2, MEMBERS, PADDED, XTRACK), jnp.bfloat16),
            pltpu.VMEM((2, MEMBERS, PADDED, XTRACK), jnp.bfloat16),
            pltpu.VMEM((LINES, PADDED, XTRACK), jnp.bfloat16),
            dma((2,)),
            dma((2,)),
            dma((2,)),
            dma((80,)),
            dma((80,)),
            dma((2,)),
            dma((2,)),
            dma((MEMBERS,)),
            dma((MEMBERS,)),
            dma((MEMBERS,)),
            dma((MEMBERS,)),
            dma((4,)),
            dma((MEMBERS,)),
        ],
        compiler_params=pltpu.CompilerParams(collective_id=0, has_side_effects=True),
    )(
        grid_profiles,
        send_lists[0],
        counts,
        angle_index[None, :],
        jacobian.transpose(0, 2, 1),
        observed,
        kappa,
        factor,
    )
    return weighted.astype(jnp.float32)


def solution(mesh):
    in_specs = (
        P("swath", None),
        P("swath", None, None),
        P("swath", None),
        P(),
        P(None, None, "chan"),
        P("chan", "swath"),
        P(None, "chan"),
        P("chan", None),
    )
    out_specs = P("chan", "swath")
    return jax.shard_map(
        on_device, mesh=mesh, in_specs=in_specs, out_specs=out_specs, check_vma=False
    )
```

```python
import functools
import math

import jax
import jax.numpy as jnp
from jax import lax
from jax.experimental import pallas as pl
from jax.experimental.pallas import tpu as pltpu
from jax.sharding import PartitionSpec as P

XTRACK = 128
NANG = 8
SWEEPS = 3
SIDE = 4
MEMBERS = SIDE * SIDE
SWATHS = 2 * MEMBERS
LINES = 32
DEPTH = 256
PADDED = 48
ROWS = 40
GROUP = 4
PARTS = 2
MESH = pl.DeviceIdType.MESH

max_zenith = math.pi / 3.0


def kernel(
    own_chan,
    grid_in,
    lists,
    counts,
    angle,
    jac_held,
    observed_in,
    kappa,
    factor_held,
    result,
    grid,
    jac_in,
    observed,
    factor_in,
    out,
    outgoing,
    own_factor,
    jac,
    weights,
    profiles,
    factor,
    field,
    field_1,
    field_2,
    smoothed,
    every,
    product,
    arrived,
    slot_send,
    slot_recv,
    slot_local,
    ring_send,
    ring_recv,
    edge_send,
    edge_recv,
    there_send,
    there_recv,
    back_send,
    back_recv,
    load_sem,
    store_sem,
):
    swath = lax.axis_index("swath")
    chan = lax.axis_index("chan")
    x, y = chan // SIDE, chan % SIDE
    above = lax.rem(swath + 1, SWATHS)
    below = lax.rem(swath + SWATHS - 1, SWATHS)

    def member(route, first, second):
        dx, dy = (first, second) if route == 0 else (second, first)
        return lax.rem(x + dx + SIDE, SIDE) * SIDE + lax.rem(y + dy + SIDE, SIDE)

    def line_of(route, who):
        return lax.rem(who + SWATHS - swath, MEMBERS) + MEMBERS * route

    partners = [line_of(k, chan) for k in range(2)]

    field[...] = jnp.zeros(field.shape, jnp.float32)
    barrier = pltpu.get_barrier_semaphore()
    for i in range(1, MEMBERS):
        other = lax.rem(chan + i, MEMBERS)
        pl.semaphore_signal(barrier, inc=1, device_id={"chan": other}, device_id_type=MESH)
    for other in (above, below):
        pl.semaphore_signal(barrier, inc=1, device_id={"swath": other}, device_id_type=MESH)
    for other in partners:

        @pl.when(other != swath)
        def _():
            pl.semaphore_signal(barrier, inc=1, device_id={"swath": other}, device_id_type=MESH)

    loads = [
        pltpu.make_async_copy(held, block, load_sem.at[i])
        for i, (held, block) in enumerate(
            ((grid_in, grid), (factor_held, factor_in), (jac_held, jac_in), (observed_in, observed))
        )
    ]
    for load in loads:
        load.start()

    loads[0].wait()
    grid_rows = grid.shape[0]
    slot = lax.broadcasted_iota(jnp.int32, (1, XTRACK), 1)
    grid_row = lax.broadcasted_iota(jnp.int32, (grid_rows, XTRACK), 0)
    for k in range(2):
        picked = lists[pl.ds(partners[k], 1), :]
        picked = jnp.where(slot < counts[0, partners[k]], picked, -1)
        chosen = jnp.where(grid_row == picked, 1.0, 0.0).astype(jnp.bfloat16)
        outgoing[k] = lax.dot_general(
            chosen, grid[...], (((0,), (0,)), ((), ())), preferred_element_type=jnp.float32
        ).astype(jnp.bfloat16)

    channels = MEMBERS * own_chan
    place = lax.broadcasted_iota(jnp.int32, (1, MEMBERS * PADDED), 1)
    owner = sum(jnp.where(place >= m * PADDED, 1, 0) for m in range(1, MEMBERS))
    target = jnp.where(place - owner * PADDED < own_chan, place - owner * (PADDED - own_chan), -1)
    source_row = lax.broadcasted_iota(jnp.int32, (channels, MEMBERS * PADDED), 0)
    spread = jnp.where(source_row == target, 1.0, 0.0).astype(jnp.bfloat16)
    loads[1].wait()
    spaced = jnp.dot(factor_in[...], spread, preferred_element_type=jnp.float32)
    spaced = spaced.astype(jnp.bfloat16)
    half_depth = MEMBERS * PADDED // 2
    own_factor[...] = jnp.zeros(own_factor.shape, jnp.bfloat16)
    for k in range(2):
        own_factor[k, pl.ds(0, own_chan)] = spaced[:, k * half_depth : (k + 1) * half_depth]

    loads[2].wait()
    loads[3].wait()
    jac[...] = jnp.zeros(jac.shape, jnp.bfloat16)
    for m in range(3):
        jac[pl.ds(m * PADDED, own_chan)] = jac_in[m]

    smoothed[...] = jnp.zeros(smoothed.shape, jnp.bfloat16)

    distinct = sum(jnp.where(other != swath, 1, 0) for other in partners)
    pl.semaphore_wait(barrier, MEMBERS + 1 + distinct)

    part_rows = XTRACK // PARTS

    def part_of(block, part):
        return block.at[pl.ds(part * part_rows, part_rows)]

    def slot_copy(k, part, half):
        return pltpu.make_async_remote_copy(
            src_ref=part_of(outgoing.at[k], part),
            dst_ref=part_of(profiles.at[swath], part),
            send_sem=slot_send.at[k * PARTS + part],
            recv_sem=slot_recv.at[half * PARTS + part],
            device_id={"swath": partners[k]},
            device_id_type=MESH,
        )

    def slot_kept(k, part):
        return pltpu.make_async_copy(
            part_of(outgoing.at[k], part),
            part_of(profiles.at[swath], part),
            slot_local.at[k * PARTS + part],
        )

    for part in range(PARTS):
        for k in range(2):

            @pl.when(partners[k] != swath)
            def _():
                slot_copy(k, part, swath // MEMBERS).start()

            @pl.when(partners[k] == swath)
            def _():
                slot_kept(k, part).start()

    def profile_piece(part, route, who):
        return part_of(profiles.at[line_of(route, who)], part)

    def profile_half(part, route, who, half):
        rows = part_rows // 2
        start = part * part_rows + half * rows
        return profiles.at[line_of(route, who), pl.ds(start, rows)]

    def factor_piece(route, who):
        return factor.at[route, who]

    def factor_half(route, who, half):
        return factor.at[route, who, pl.ds(0, 32) if half == 0 else pl.ds(32, 16)]

    sent = []
    offsets = (0, -1, 1, 2)

    class Ring:
        def __init__(self, kind, route, piece, half):
            self.kind, self.route, self.piece, self.half = kind, route, piece, half
            self.copies = {}

        def send(self, key, number, source, target, to):
            at = self.kind * 20 + number
            copy = pltpu.make_async_remote_copy(
                src_ref=source,
                dst_ref=target,
                send_sem=ring_send.at[at],
                recv_sem=ring_recv.at[at],
                device_id={"chan": to},
                device_id_type=MESH,
            )
            copy.start()
            sent.append(copy)
            self.copies[key] = copy

        def whole(self, offset, source=None):
            who = member(self.route, offset, 0)
            target = self.piece(self.route, who)
            for way in range(2):
                to = member(self.route, 0, 1 - 2 * way)
                number = 4 + offsets.index(offset) * 2 + way
                self.send(("b", offset, way), number, target if source is None else source, target, to)

        def open(self, source=None):
            target = self.piece(self.route, chan)
            for way in range(2):
                to = member(self.route, 1 - 2 * way, 0)
                self.send(("a", way), way, target if source is None else source, target, to)
            to = member(self.route, 2, 0)
            self.send(("c", 0), 2, target if source is None else source, target, to)
            self.whole(0, source)

        def relay(self):
            for way in range(2):
                self.copies["a", way].wait_recv()
                came = 2 * way - 1
                self.whole(came)

        def across(self):
            self.copies["c", 0].wait_recv()
            self.whole(2)

        def finish(self):
            for index, offset in enumerate(offsets):
                for way in range(2):
                    self.copies["b", offset, way].wait_recv()
                    came = 2 * way - 1
                    part = self.half(self.route, member(self.route, offset, came), way)
                    number = 12 + index * 2 + way
                    self.send(("d", offset, way), number, part, part, member(self.route, 0, -came))

        def close(self):
            for offset in offsets:
                for way in range(2):
                    self.copies["d", offset, way].wait_recv()

    factor_rings = [Ring(k, k, factor_piece, factor_half) for k in range(2)]
    profile_rings = [
        Ring(
            2 + part * 2 + k,
            k,
            functools.partial(profile_piece, part),
            functools.partial(profile_half, part),
        )
        for part in range(PARTS)
        for k in range(2)
    ]

    for k, ring in enumerate(factor_rings):
        ring.open(own_factor.at[k])
    for k in range(2):
        factor[k, chan] = own_factor[k]
    for ring in factor_rings:
        ring.relay()
    for ring in factor_rings:
        ring.across()
    for i, ring in enumerate(profile_rings):
        part, k = i // 2, i % 2

        @pl.when(partners[k] != swath)
        def _():
            slot_copy(k, part, k).wait_recv()

        @pl.when(partners[k] == swath)
        def _():
            slot_kept(k, part).wait()

        ring.open()
    for ring in profile_rings:
        ring.relay()
    for ring in profile_rings:
        ring.across()
    for ring in profile_rings:
        ring.finish()
    for ring in factor_rings:
        ring.finish()
    zenith = angle[...].astype(jnp.float32) * (max_zenith / (NANG - 1))
    path = 1.0 / jnp.cos(zenith) - 1.0
    path_2 = path * path

    def depart(route, first, second):
        line = line_of(route, member(route, first, second))
        model = lax.dot_general(
            jac[...], profiles[line], (((1,), (1,)), ((), ())), preferred_element_type=jnp.float32
        )
        columns = pl.ds(pl.multiple_of(line * XTRACK, XTRACK), XTRACK)
        value = (
            model[:PADDED]
            + path * model[PADDED : 2 * PADDED]
            + path_2 * model[2 * PADDED :]
        )
        field[line + SWEEPS, pl.ds(0, own_chan)] = (
            observed[:, columns].astype(jnp.float32) - value[:own_chan]
        )

    @pl.loop(0, 3)
    def _(i):
        for route in range(2):
            for first in offsets:
                depart(route, first, i - 1)

    for ring in profile_rings:
        ring.close()
    for route in range(2):
        for first in offsets:
            depart(route, first, 2)

    column = lax.broadcasted_iota(jnp.int32, (ROWS, XTRACK), 1)
    on_diagonal = lax.broadcasted_iota(jnp.int32, (ROWS, own_chan), 0) == (
        lax.broadcasted_iota(jnp.int32, (ROWS, own_chan), 1)
    )
    spread_rates = [
        jnp.broadcast_to(
            jnp.sum(jnp.where(on_diagonal, kappa[pl.ds(k, 1), :], 0.0), axis=1, keepdims=True),
            (ROWS, XTRACK),
        )
        for k in range(2)
    ]
    weights[0] = 1.0 - 2.0 * (spread_rates[0] + spread_rates[1])
    weights[1] = spread_rates[0]
    weights[2] = jnp.where(column == 0, 0.0, spread_rates[1])
    weights[3] = jnp.where(column == XTRACK - 1, 0.0, spread_rates[1])

    edges = []
    for way, (source, target, to) in enumerate(
        ((LINES, 0, above), (SWEEPS, LINES + SWEEPS, below))
    ):
        copy = pltpu.make_async_remote_copy(
            src_ref=field.at[pl.ds(source, SWEEPS)],
            dst_ref=field.at[pl.ds(target, SWEEPS)],
            send_sem=edge_send.at[way],
            recv_sem=edge_recv.at[way],
            device_id={"swath": to},
            device_id_type=MESH,
        )
        copy.start()
        edges.append(copy)
        sent.append(copy)

    def clear(block, width):
        @pl.when(swath == 0)
        def _():
            block[pl.ds(0, width)] = jnp.zeros((width, ROWS, XTRACK), jnp.float32)

        @pl.when(swath == SWATHS - 1)
        def _():
            block[pl.ds(LINES + width, width)] = jnp.zeros((width, ROWS, XTRACK), jnp.float32)

    weight = [weights[k] for k in range(4)]

    def diffuse(block, at):
        center = block[at]
        left = pltpu.roll(center, 1, 1)
        right = pltpu.roll(center, XTRACK - 1, 1)
        return (
            weight[0] * center
            + weight[1] * (block[at + 1] + block[at - 1])
            + (weight[2] * left + weight[3] * right)
        )

    def sweep(source, target, start, count, step):
        @pl.loop(0, count // step)
        def _(turn):
            for i in range(step):
                at = start + step * turn + i
                target[at] = diffuse(source, at + 1)

        for at in range(start + count - count % step, start + count):
            target[at] = diffuse(source, at + 1)

    def there(who, into):
        return pltpu.make_async_remote_copy(
            src_ref=smoothed.at[pl.ds(2 * who, 2)],
            dst_ref=every.at[:, into],
            send_sem=there_send.at[who],
            recv_sem=there_recv.at[into],
            device_id={"chan": who},
            device_id_type=MESH,
        )

    def smooth_pair(who):
        for j in range(2):
            value = diffuse(field_2, 2 * who + j + 1).astype(jnp.bfloat16)
            smoothed[2 * who + j, pl.ds(0, ROWS)] = value

    def send_pair(who):
        @pl.when(who != chan)
        def _():
            there(who, chan).start()

    inner = MEMBERS - 4

    def inner_member(i):
        return 2 + lax.rem(chan + i, inner)

    sweep(field, field_1, SWEEPS, LINES - 2, 6)
    sweep(field_1, field_2, SWEEPS, LINES - 4, 7)
    smooth_pair(inner_member(0))

    @pl.loop(1, inner)
    def _(i):
        smooth_pair(inner_member(i))
        send_pair(inner_member(i - 1))

    for copy in edges:
        copy.wait_recv()
    clear(field, 3)
    for start in (0, LINES + 1):
        sweep(field, field_1, start, 3, 3)
    clear(field_1, 2)
    for start in (0, LINES - 1):
        sweep(field_1, field_2, start, 3, 3)
    clear(field_2, 1)
    send_pair(inner_member(inner - 1))
    outer = (0, MEMBERS - 1, 1, MEMBERS - 2)
    for who in outer:
        smooth_pair(who)
    for who in outer:
        send_pair(who)

    for j in range(2):
        every[j, chan] = smoothed[2 * chan + j]

    @pl.loop(1, MEMBERS)
    def _(i):
        who = lax.rem(chan + i, MEMBERS)
        there(who, who).wait_recv()

    for ring in factor_rings:
        ring.close()

    pieces = [every[j].reshape(MEMBERS * PADDED, XTRACK) for j in range(2)]
    wide = jnp.concatenate(pieces, axis=1)

    def weigh(group):
        rows = [
            factor[k, pl.ds(group * GROUP, GROUP)].reshape(GROUP * PADDED, half_depth)
            for k in range(2)
        ]
        block = jnp.dot(
            rows[0], wide[:half_depth], preferred_element_type=jnp.float32
        ) + jnp.dot(rows[1], wide[half_depth:], preferred_element_type=jnp.float32)
        for j in range(2):
            part = block[:, j * XTRACK : (j + 1) * XTRACK].astype(jnp.bfloat16)
            product[j, pl.ds(group * GROUP, GROUP)] = part.reshape(GROUP, PADDED, XTRACK)

    def back(who, into):
        return pltpu.make_async_remote_copy(
            src_ref=product.at[:, who],
            dst_ref=arrived.at[pl.ds(2 * into, 2)],
            send_sem=back_send.at[who],
            recv_sem=back_recv.at[into],
            device_id={"chan": who},
            device_id_type=MESH,
        )

    groups = MEMBERS // GROUP

    def group_at(i):
        return lax.rem(chan // GROUP + 1 + i, groups)

    def send_group(group):
        for i in range(GROUP):
            who = group * GROUP + lax.rem(chan + i, GROUP)

            @pl.when(who != chan)
            def _():
                back(who, chan).start()

    for i in range(groups):
        weigh(group_at(i))
        if i > 0:
            send_group(group_at(i - 1))
    send_group(group_at(groups - 1))

    for j in range(2):
        arrived[2 * chan + j] = product[j, chan]

    def settle(who):
        for j in range(2):
            at = 2 * who + j
            columns = pl.ds(pl.multiple_of(at * XTRACK, XTRACK), XTRACK)
            out[:, columns] = arrived[at, pl.ds(0, own_chan)]

    def store(who):
        columns = pl.ds(pl.multiple_of(2 * who * XTRACK, 2 * XTRACK), 2 * XTRACK)
        return pltpu.make_async_copy(
            out.at[:, columns], result.at[:, columns], store_sem.at[who]
        )

    settle(chan)

    @pl.loop(1, MEMBERS)
    def _(i):
        who = lax.rem(chan + i, MEMBERS)
        back(who, who).wait_recv()
        settle(who)
        store(lax.rem(chan + i - 1, MEMBERS)).start()

    for copy in sent:
        copy.wait_send()
    for k in range(2):

        @pl.when(partners[k] != swath)
        def _():
            for part in range(PARTS):
                slot_copy(k, part, k).wait_send()

    store(lax.rem(chan + MEMBERS - 1, MEMBERS)).start()

    @pl.loop(1, MEMBERS)
    def _(i):
        who = lax.rem(chan + i, MEMBERS)
        there(who, chan).wait_send()
        back(who, chan).wait_send()

    @pl.loop(0, MEMBERS)
    def _(who):
        store(who).wait()


def on_device(grid_profiles, send_lists, counts, angle_index, jacobian, observed, kappa, factor):
    own_chan = observed.shape[0]
    pixel_count = observed.shape[1]
    half_depth = MEMBERS * PADDED // 2
    vmem = pl.BlockSpec(memory_space=pltpu.VMEM)
    held = pl.BlockSpec(memory_space=pl.ANY)
    dma = pltpu.SemaphoreType.DMA
    weighted = pl.pallas_call(
        functools.partial(kernel, own_chan),
        out_shape=jax.ShapeDtypeStruct((own_chan, pixel_count), jnp.bfloat16),
        in_specs=[held, vmem, pl.BlockSpec(memory_space=pltpu.SMEM), vmem, held, held, vmem, held],
        out_specs=held,
        scratch_shapes=[
            pltpu.VMEM(grid_profiles.shape, jnp.bfloat16),
            pltpu.VMEM((3, own_chan, DEPTH), jnp.bfloat16),
            pltpu.VMEM(observed.shape, jnp.bfloat16),
            pltpu.VMEM(factor.shape, jnp.bfloat16),
            pltpu.VMEM(observed.shape, jnp.bfloat16),
            pltpu.VMEM((2, XTRACK, DEPTH), jnp.bfloat16),
            pltpu.VMEM((2, PADDED, half_depth), jnp.bfloat16),
            pltpu.VMEM((3 * PADDED, DEPTH), jnp.bfloat16),
            pltpu.VMEM((4, ROWS, XTRACK), jnp.float32),
            pltpu.VMEM((LINES, XTRACK, DEPTH), jnp.bfloat16),
            pltpu.VMEM((2, MEMBERS, PADDED, half_depth), jnp.bfloat16),
            pltpu.VMEM((LINES + 6, ROWS, XTRACK), jnp.float32),
            pltpu.VMEM((LINES + 4, ROWS, XTRACK), jnp.float32),
            pltpu.VMEM((LINES + 2, ROWS, XTRACK), jnp.float32),
            pltpu.VMEM((LINES, PADDED, XTRACK), jnp.bfloat16),
            pltpu.VMEM((2, MEMBERS, PADDED, XTRACK), jnp.bfloat16),
            pltpu.VMEM((2, MEMBERS, PADDED, XTRACK), jnp.bfloat16),
            pltpu.VMEM((LINES, PADDED, XTRACK), jnp.bfloat16),
            dma((2 * PARTS,)),
            dma((2 * PARTS,)),
            dma((2 * PARTS,)),
            dma((40 + 40 * PARTS,)),
            dma((40 + 40 * PARTS,)),
            dma((2,)),
            dma((2,)),
            dma((MEMBERS,)),
            dma((MEMBERS,)),
            dma((MEMBERS,)),
            dma((MEMBERS,)),
            dma((4,)),
            dma((MEMBERS,)),
        ],
        compiler_params=pltpu.CompilerParams(collective_id=0, has_side_effects=True),
    )(
        grid_profiles,
        send_lists[0],
        counts,
        angle_index[None, :],
        jacobian.transpose(0, 2, 1),
        observed,
        kappa,
        factor,
    )
    return weighted.astype(jnp.float32)


def solution(mesh):
    in_specs = (
        P("swath", None),
        P("swath", None, None),
        P("swath", None),
        P(),
        P(None, None, "chan"),
        P("chan", "swath"),
        P(None, "chan"),
        P("chan", None),
    )
    out_specs = P("chan", "swath")
    return jax.shard_map(
        on_device, mesh=mesh, in_specs=in_specs, out_specs=out_specs, check_vma=False
    )
```

```python
import functools
import math

import jax
import jax.numpy as jnp
from jax import lax
from jax.experimental import pallas as pl
from jax.experimental.pallas import tpu as pltpu
from jax.sharding import PartitionSpec as P

XTRACK = 128
NANG = 8
SWEEPS = 3
SIDE = 4
MEMBERS = SIDE * SIDE
SWATHS = 2 * MEMBERS
LINES = 32
DEPTH = 256
PADDED = 48
ROWS = 40
GROUP = 4
PARTS = 2
MESH = pl.DeviceIdType.MESH

max_zenith = math.pi / 3.0


def kernel(
    own_chan,
    grid_in,
    lists,
    counts,
    angle,
    jac_held,
    observed_in,
    kappa,
    factor_held,
    result,
    grid,
    jac_in,
    observed,
    factor_in,
    out,
    outgoing,
    own_factor,
    jac,
    weights,
    profiles,
    factor,
    field,
    field_1,
    field_2,
    smoothed,
    every,
    product,
    arrived,
    slot_send,
    slot_recv,
    slot_local,
    ring_send,
    ring_recv,
    edge_send,
    edge_recv,
    there_send,
    there_recv,
    back_send,
    back_recv,
    load_sem,
    store_sem,
):
    swath = lax.axis_index("swath")
    chan = lax.axis_index("chan")
    x, y = chan // SIDE, chan % SIDE
    above = lax.rem(swath + 1, SWATHS)
    below = lax.rem(swath + SWATHS - 1, SWATHS)

    def member(route, first, second):
        dx, dy = (first, second) if route == 0 else (second, first)
        return lax.rem(x + dx + SIDE, SIDE) * SIDE + lax.rem(y + dy + SIDE, SIDE)

    def line_of(route, who):
        return lax.rem(who + SWATHS - swath, MEMBERS) + MEMBERS * route

    partners = [line_of(k, chan) for k in range(2)]

    field[...] = jnp.zeros(field.shape, jnp.float32)
    barrier = pltpu.get_barrier_semaphore()
    for i in range(1, MEMBERS):
        other = lax.rem(chan + i, MEMBERS)
        pl.semaphore_signal(barrier, inc=1, device_id={"chan": other}, device_id_type=MESH)
    for other in (above, below):
        pl.semaphore_signal(barrier, inc=1, device_id={"swath": other}, device_id_type=MESH)
    for other in partners:

        @pl.when(other != swath)
        def _():
            pl.semaphore_signal(barrier, inc=1, device_id={"swath": other}, device_id_type=MESH)

    loads = [
        pltpu.make_async_copy(held, block, load_sem.at[i])
        for i, (held, block) in enumerate(
            ((grid_in, grid), (factor_held, factor_in), (jac_held, jac_in), (observed_in, observed))
        )
    ]
    for load in loads:
        load.start()

    loads[0].wait()
    grid_rows = grid.shape[0]
    slot = lax.broadcasted_iota(jnp.int32, (1, XTRACK), 1)
    grid_row = lax.broadcasted_iota(jnp.int32, (grid_rows, XTRACK), 0)
    for k in range(2):
        picked = lists[pl.ds(partners[k], 1), :]
        picked = jnp.where(slot < counts[0, partners[k]], picked, -1)
        chosen = jnp.where(grid_row == picked, 1.0, 0.0).astype(jnp.bfloat16)
        outgoing[k] = lax.dot_general(
            chosen, grid[...], (((0,), (0,)), ((), ())), preferred_element_type=jnp.float32
        ).astype(jnp.bfloat16)

    channels = MEMBERS * own_chan
    place = lax.broadcasted_iota(jnp.int32, (1, MEMBERS * ROWS), 1)
    owner = sum(jnp.where(place >= m * ROWS, 1, 0) for m in range(1, MEMBERS))
    target = jnp.where(place - owner * ROWS < own_chan, place - owner * (ROWS - own_chan), -1)
    source_row = lax.broadcasted_iota(jnp.int32, (channels, MEMBERS * ROWS), 0)
    spread = jnp.where(source_row == target, 1.0, 0.0).astype(jnp.bfloat16)
    loads[1].wait()
    spaced = jnp.dot(factor_in[...], spread, preferred_element_type=jnp.float32)
    spaced = spaced.astype(jnp.bfloat16)
    half_depth = MEMBERS * PADDED // 2
    own_factor[...] = jnp.zeros(own_factor.shape, jnp.bfloat16)
    for k in range(2):
        first = k * (MEMBERS * ROWS - half_depth)
        own_factor[k, pl.ds(0, own_chan)] = spaced[:, first : first + half_depth]

    loads[2].wait()
    loads[3].wait()
    jac[...] = jnp.zeros(jac.shape, jnp.bfloat16)
    for m in range(3):
        jac[pl.ds(m * PADDED, own_chan)] = jac_in[m]

    distinct = sum(jnp.where(other != swath, 1, 0) for other in partners)
    pl.semaphore_wait(barrier, MEMBERS + 1 + distinct)

    part_rows = XTRACK // PARTS

    def part_of(block, part):
        return block.at[pl.ds(part * part_rows, part_rows)]

    def slot_copy(k, part, half):
        return pltpu.make_async_remote_copy(
            src_ref=part_of(outgoing.at[k], part),
            dst_ref=part_of(profiles.at[swath], part),
            send_sem=slot_send.at[k * PARTS + part],
            recv_sem=slot_recv.at[half * PARTS + part],
            device_id={"swath": partners[k]},
            device_id_type=MESH,
        )

    def slot_kept(k, part):
        return pltpu.make_async_copy(
            part_of(outgoing.at[k], part),
            part_of(profiles.at[swath], part),
            slot_local.at[k * PARTS + part],
        )

    for part in range(PARTS):
        for k in range(2):

            @pl.when(partners[k] != swath)
            def _():
                slot_copy(k, part, swath // MEMBERS).start()

            @pl.when(partners[k] == swath)
            def _():
                slot_kept(k, part).start()

    def profile_piece(part, route, who):
        return part_of(profiles.at[line_of(route, who)], part)

    def profile_half(part, route, who, half):
        rows = part_rows // 2
        start = part * part_rows + half * rows
        return profiles.at[line_of(route, who), pl.ds(start, rows)]

    def factor_piece(route, who):
        return factor.at[route, who]

    def factor_half(route, who, half):
        return factor.at[route, who, pl.ds(0, 32) if half == 0 else pl.ds(32, 16)]

    sent = []
    offsets = (0, -1, 1, 2)

    class Ring:
        def __init__(self, kind, route, piece, half):
            self.kind, self.route, self.piece, self.half = kind, route, piece, half
            self.copies = {}

        def send(self, key, number, source, target, to):
            at = self.kind * 20 + number
            copy = pltpu.make_async_remote_copy(
                src_ref=source,
                dst_ref=target,
                send_sem=ring_send.at[at],
                recv_sem=ring_recv.at[at],
                device_id={"chan": to},
                device_id_type=MESH,
            )
            copy.start()
            sent.append(copy)
            self.copies[key] = copy

        def whole(self, offset, source=None):
            who = member(self.route, offset, 0)
            target = self.piece(self.route, who)
            for way in range(2):
                to = member(self.route, 0, 1 - 2 * way)
                number = 4 + offsets.index(offset) * 2 + way
                self.send(("b", offset, way), number, target if source is None else source, target, to)

        def open(self, source=None):
            target = self.piece(self.route, chan)
            for way in range(2):
                to = member(self.route, 1 - 2 * way, 0)
                self.send(("a", way), way, target if source is None else source, target, to)
            to = member(self.route, 2, 0)
            self.send(("c", 0), 2, target if source is None else source, target, to)
            self.whole(0, source)

        def relay(self):
            for way in range(2):
                self.copies["a", way].wait_recv()
                came = 2 * way - 1
                self.whole(came)

        def across(self):
            self.copies["c", 0].wait_recv()
            self.whole(2)

        def finish(self):
            for index, offset in enumerate(offsets):
                for way in range(2):
                    self.copies["b", offset, way].wait_recv()
                    came = 2 * way - 1
                    part = self.half(self.route, member(self.route, offset, came), way)
                    number = 12 + index * 2 + way
                    self.send(("d", offset, way), number, part, part, member(self.route, 0, -came))

        def close(self):
            for offset in offsets:
                for way in range(2):
                    self.copies["d", offset, way].wait_recv()

    factor_rings = [Ring(k, k, factor_piece, factor_half) for k in range(2)]
    profile_rings = [
        Ring(
            2 + part * 2 + k,
            k,
            functools.partial(profile_piece, part),
            functools.partial(profile_half, part),
        )
        for part in range(PARTS)
        for k in range(2)
    ]

    for k, ring in enumerate(factor_rings):
        ring.open(own_factor.at[k])
    for k in range(2):
        factor[k, chan] = own_factor[k]
    for ring in factor_rings:
        ring.relay()
    for ring in factor_rings:
        ring.across()
    for i, ring in enumerate(profile_rings):
        part, k = i // 2, i % 2

        @pl.when(partners[k] != swath)
        def _():
            slot_copy(k, part, k).wait_recv()

        @pl.when(partners[k] == swath)
        def _():
            slot_kept(k, part).wait()

        ring.open()
    for ring in profile_rings:
        ring.relay()
    for ring in profile_rings:
        ring.across()
    for ring in profile_rings:
        ring.finish()
    for ring in factor_rings:
        ring.finish()
    zenith = angle[...].astype(jnp.float32) * (max_zenith / (NANG - 1))
    path = 1.0 / jnp.cos(zenith) - 1.0
    path_2 = path * path

    def depart(route, first, second):
        line = line_of(route, member(route, first, second))
        model = lax.dot_general(
            jac[...], profiles[line], (((1,), (1,)), ((), ())), preferred_element_type=jnp.float32
        )
        columns = pl.ds(pl.multiple_of(line * XTRACK, XTRACK), XTRACK)
        value = (
            model[:PADDED]
            + path * model[PADDED : 2 * PADDED]
            + path_2 * model[2 * PADDED :]
        )
        field[line + SWEEPS, pl.ds(0, own_chan)] = (
            observed[:, columns].astype(jnp.float32) - value[:own_chan]
        )

    @pl.loop(0, 3)
    def _(i):
        for route in range(2):
            for first in offsets:
                depart(route, first, i - 1)

    for ring in profile_rings:
        ring.close()
    for route in range(2):
        for first in offsets:
            depart(route, first, 2)

    column = lax.broadcasted_iota(jnp.int32, (ROWS, XTRACK), 1)
    on_diagonal = lax.broadcasted_iota(jnp.int32, (ROWS, own_chan), 0) == (
        lax.broadcasted_iota(jnp.int32, (ROWS, own_chan), 1)
    )
    spread_rates = [
        jnp.broadcast_to(
            jnp.sum(jnp.where(on_diagonal, kappa[pl.ds(k, 1), :], 0.0), axis=1, keepdims=True),
            (ROWS, XTRACK),
        )
        for k in range(2)
    ]
    weights[0] = 1.0 - 2.0 * (spread_rates[0] + spread_rates[1])
    weights[1] = spread_rates[0]
    weights[2] = jnp.where(column == 0, 0.0, spread_rates[1])
    weights[3] = jnp.where(column == XTRACK - 1, 0.0, spread_rates[1])

    edges = []
    for way, (source, target, to) in enumerate(
        ((LINES, 0, above), (SWEEPS, LINES + SWEEPS, below))
    ):
        copy = pltpu.make_async_remote_copy(
            src_ref=field.at[pl.ds(source, SWEEPS)],
            dst_ref=field.at[pl.ds(target, SWEEPS)],
            send_sem=edge_send.at[way],
            recv_sem=edge_recv.at[way],
            device_id={"swath": to},
            device_id_type=MESH,
        )
        copy.start()
        edges.append(copy)
        sent.append(copy)

    def clear(block, width):
        @pl.when(swath == 0)
        def _():
            block[pl.ds(0, width)] = jnp.zeros((width, ROWS, XTRACK), jnp.float32)

        @pl.when(swath == SWATHS - 1)
        def _():
            block[pl.ds(LINES + width, width)] = jnp.zeros((width, ROWS, XTRACK), jnp.float32)

    weight = [weights[k] for k in range(4)]

    def diffuse(block, at):
        center = block[at]
        left = pltpu.roll(center, 1, 1)
        right = pltpu.roll(center, XTRACK - 1, 1)
        return (
            weight[0] * center
            + weight[1] * (block[at + 1] + block[at - 1])
            + (weight[2] * left + weight[3] * right)
        )

    def sweep(source, target, start, count, step):
        @pl.loop(0, count // step)
        def _(turn):
            for i in range(step):
                at = start + step * turn + i
                target[at] = diffuse(source, at + 1)

        for at in range(start + count - count % step, start + count):
            target[at] = diffuse(source, at + 1)

    def there(who, into):
        return pltpu.make_async_remote_copy(
            src_ref=smoothed.at[who],
            dst_ref=every.at[into],
            send_sem=there_send.at[who],
            recv_sem=there_recv.at[into],
            device_id={"chan": who},
            device_id_type=MESH,
        )

    def smooth_pair(who):
        pair = [diffuse(field_2, 2 * who + j + 1) for j in range(2)]
        smoothed[who] = jnp.concatenate(pair, axis=0).astype(jnp.bfloat16)

    def send_pair(who):
        @pl.when(who != chan)
        def _():
            there(who, chan).start()

    inner = MEMBERS - 4

    def inner_member(i):
        return 2 + lax.rem(chan + i, inner)

    sweep(field, field_1, SWEEPS, LINES - 2, 6)
    sweep(field_1, field_2, SWEEPS, LINES - 4, 7)
    smooth_pair(inner_member(0))

    @pl.loop(1, inner)
    def _(i):
        smooth_pair(inner_member(i))
        send_pair(inner_member(i - 1))

    for copy in edges:
        copy.wait_recv()
    clear(field, 3)
    for start in (0, LINES + 1):
        sweep(field, field_1, start, 3, 3)
    clear(field_1, 2)
    for start in (0, LINES - 1):
        sweep(field_1, field_2, start, 3, 3)
    clear(field_2, 1)
    send_pair(inner_member(inner - 1))
    outer = (0, MEMBERS - 1, 1, MEMBERS - 2)
    for who in outer:
        smooth_pair(who)
    for who in outer:
        send_pair(who)

    every[chan] = smoothed[chan]

    @pl.loop(1, MEMBERS)
    def _(i):
        who = lax.rem(chan + i, MEMBERS)
        there(who, who).wait_recv()

    for ring in factor_rings:
        ring.close()

    pairs = [every[m].astype(jnp.float32) for m in range(MEMBERS)]
    wide = jnp.concatenate(
        [jnp.concatenate([pair[:ROWS], pair[ROWS:]], axis=1) for pair in pairs], axis=0
    ).astype(jnp.bfloat16)
    overlap = 2 * half_depth - MEMBERS * ROWS

    def weigh(group):
        rows = [
            factor[k, pl.ds(group * GROUP, GROUP)].reshape(GROUP * PADDED, half_depth)
            for k in range(2)
        ]
        block = jnp.dot(
            rows[0], wide[:half_depth], preferred_element_type=jnp.float32
        ) + jnp.dot(
            rows[1][:, overlap:], wide[half_depth:], preferred_element_type=jnp.float32
        )
        for i in range(GROUP):
            part = block[i * PADDED : i * PADDED + ROWS]
            product[group * GROUP + i] = jnp.concatenate(
                [part[:, :XTRACK], part[:, XTRACK:]], axis=0
            ).astype(jnp.bfloat16)

    def back(who, into):
        return pltpu.make_async_remote_copy(
            src_ref=product.at[who],
            dst_ref=arrived.at[into],
            send_sem=back_send.at[who],
            recv_sem=back_recv.at[into],
            device_id={"chan": who},
            device_id_type=MESH,
        )

    groups = MEMBERS // GROUP

    def group_at(i):
        return lax.rem(chan // GROUP + 1 + i, groups)

    def send_group(group):
        for i in range(GROUP):
            who = group * GROUP + lax.rem(chan + i, GROUP)

            @pl.when(who != chan)
            def _():
                back(who, chan).start()

    for i in range(groups):
        weigh(group_at(i))
        if i > 0:
            send_group(group_at(i - 1))
    send_group(group_at(groups - 1))

    arrived[chan] = product[chan]

    def settle(who):
        pair = arrived[who].astype(jnp.float32)
        for j in range(2):
            columns = pl.ds(pl.multiple_of((2 * who + j) * XTRACK, XTRACK), XTRACK)
            out[:, columns] = pair[j * ROWS : j * ROWS + own_chan].astype(jnp.bfloat16)

    def store(who):
        columns = pl.ds(pl.multiple_of(2 * who * XTRACK, 2 * XTRACK), 2 * XTRACK)
        return pltpu.make_async_copy(
            out.at[:, columns], result.at[:, columns], store_sem.at[who]
        )

    settle(chan)

    @pl.loop(1, MEMBERS)
    def _(i):
        who = lax.rem(chan + i, MEMBERS)
        back(who, who).wait_recv()
        settle(who)
        store(lax.rem(chan + i - 1, MEMBERS)).start()

    for copy in sent:
        copy.wait_send()
    for k in range(2):

        @pl.when(partners[k] != swath)
        def _():
            for part in range(PARTS):
                slot_copy(k, part, k).wait_send()

    store(lax.rem(chan + MEMBERS - 1, MEMBERS)).start()

    @pl.loop(1, MEMBERS)
    def _(i):
        who = lax.rem(chan + i, MEMBERS)
        there(who, chan).wait_send()
        back(who, chan).wait_send()

    @pl.loop(0, MEMBERS)
    def _(who):
        store(who).wait()


def on_device(grid_profiles, send_lists, counts, angle_index, jacobian, observed, kappa, factor):
    own_chan = observed.shape[0]
    pixel_count = observed.shape[1]
    half_depth = MEMBERS * PADDED // 2
    vmem = pl.BlockSpec(memory_space=pltpu.VMEM)
    held = pl.BlockSpec(memory_space=pl.ANY)
    dma = pltpu.SemaphoreType.DMA
    weighted = pl.pallas_call(
        functools.partial(kernel, own_chan),
        out_shape=jax.ShapeDtypeStruct((own_chan, pixel_count), jnp.bfloat16),
        in_specs=[held, vmem, pl.BlockSpec(memory_space=pltpu.SMEM), vmem, held, held, vmem, held],
        out_specs=held,
        scratch_shapes=[
            pltpu.VMEM(grid_profiles.shape, jnp.bfloat16),
            pltpu.VMEM((3, own_chan, DEPTH), jnp.bfloat16),
            pltpu.VMEM(observed.shape, jnp.bfloat16),
            pltpu.VMEM(factor.shape, jnp.bfloat16),
            pltpu.VMEM(observed.shape, jnp.bfloat16),
            pltpu.VMEM((2, XTRACK, DEPTH), jnp.bfloat16),
            pltpu.VMEM((2, PADDED, half_depth), jnp.bfloat16),
            pltpu.VMEM((3 * PADDED, DEPTH), jnp.bfloat16),
            pltpu.VMEM((4, ROWS, XTRACK), jnp.float32),
            pltpu.VMEM((LINES, XTRACK, DEPTH), jnp.bfloat16),
            pltpu.VMEM((2, MEMBERS, PADDED, half_depth), jnp.bfloat16),
            pltpu.VMEM((LINES + 6, ROWS, XTRACK), jnp.float32),
            pltpu.VMEM((LINES + 4, ROWS, XTRACK), jnp.float32),
            pltpu.VMEM((LINES + 2, ROWS, XTRACK), jnp.float32),
            pltpu.VMEM((MEMBERS, 2 * ROWS, XTRACK), jnp.bfloat16),
            pltpu.VMEM((MEMBERS, 2 * ROWS, XTRACK), jnp.bfloat16),
            pltpu.VMEM((MEMBERS, 2 * ROWS, XTRACK), jnp.bfloat16),
            pltpu.VMEM((MEMBERS, 2 * ROWS, XTRACK), jnp.bfloat16),
            dma((2 * PARTS,)),
            dma((2 * PARTS,)),
            dma((2 * PARTS,)),
            dma((40 + 40 * PARTS,)),
            dma((40 + 40 * PARTS,)),
            dma((2,)),
            dma((2,)),
            dma((MEMBERS,)),
            dma((MEMBERS,)),
            dma((MEMBERS,)),
            dma((MEMBERS,)),
            dma((4,)),
            dma((MEMBERS,)),
        ],
        compiler_params=pltpu.CompilerParams(collective_id=0, has_side_effects=True),
    )(
        grid_profiles,
        send_lists[0],
        counts,
        angle_index[None, :],
        jacobian.transpose(0, 2, 1),
        observed,
        kappa,
        factor,
    )
    return weighted.astype(jnp.float32)


def solution(mesh):
    in_specs = (
        P("swath", None),
        P("swath", None, None),
        P("swath", None),
        P(),
        P(None, None, "chan"),
        P("chan", "swath"),
        P(None, "chan"),
        P("chan", None),
    )
    out_specs = P("chan", "swath")
    return jax.shard_map(
        on_device, mesh=mesh, in_specs=in_specs, out_specs=out_specs, check_vma=False
    )
```
